32 devices in a mesh: section: 2 (over core), expert: 4 (over z), head: 4 (over y, x).
Axes of the slice: x: 2, y: 2, z: 4, core: 2. Of those that a mesh axis runs over, the one named last changes fastest.
Arguments:
- x_in: bfloat16 [1, 512, 2048], P(None, 'expert'), may hold values from -6 to 6
- cotangent: bfloat16 [1, 512, 2048], P(None, 'expert'), may hold values from -6 to 6
- segments: int32 [1, 4, 128], P(None, 'expert'), may hold values from 0 to 3, never falling along the last dimension, each value on 1 to 96 neighbouring positions
- routes: int32 [2, 1, 512, 8], P('section', None, 'expert'), may hold values from 0 to 31, all different within a row; in each aligned block of 128 rows (0 to 127, 128 to 255, ..., all dimensions but the last counted through in order) at most 40 rows name the same one
- norm1_gain: float32 [2, 2048], P('section', 'head'), may hold values from 0.1 to 1.9
- norm2_gain: float32 [2, 2048], P('section', 'head'), may hold values from 0.1 to 1.9
- q_gain: float32 [2, 128], P('section'), may hold values from 0.1 to 1.9
- k_gain: float32 [2, 128], P('section'), may hold values from 0.1 to 1.9
- w_qkv: bfloat16 [2, 3, 2048, 2048], P('section', None, None, 'head'), may hold values from -0.125 to 0.125
- w_o: bfloat16 [2, 2048, 2048], P('section', 'head'), may hold values from -0.75 to 0.75
- router: bfloat16 [2, 2048, 32], P('section', 'head'), may hold values from -0.019897461 to 0.019897461
- w_in: bfloat16 [2, 32, 2048, 2, 1024], P('section', 'expert', None, None, 'head'), may hold values from -0.125 to 0.125
- w_out: bfloat16 [2, 32, 1024, 2048], P('section', 'expert', 'head'), may hold values from -0.75 to 0.75
Outputs:
- layer_out: bfloat16 [2, 1, 512, 2048], P('section', None, 'expert')
- input_grad: bfloat16 [2, 1, 512, 2048], P('section', None, 'expert')
- norm1_grad: float32 [2, 2048], P('section', 'head')
- norm2_grad: float32 [2, 2048], P('section', 'head')
- qgain_grad: float32 [2, 128], P('section')
- kgain_grad: float32 [2, 128], P('section')
- qkv_grad: float32 [2, 3, 2048, 2048], P('section', None, 'expert', 'head')
- oproj_grad: float32 [2, 2048, 2048], P('section', 'head', 'expert')
- router_grad: float32 [2, 2048, 32], P('section', 'head')
- expin_grad: float32 [2, 32, 2048, 2, 1024], P('section', 'expert', None, None, 'head')
- expout_grad: float32 [2, 32, 1024, 2048], P('section', 'expert', 'head')
The draws below stay inside these ranges and needn't reach their ends.
Inputs may be any that keep to these rules, and one draw needn't show every extreme that they name: `routes`: in each aligned block of 128 rows (one group's tokens of one micro-batch of one layer) no expert is named by more than 40 rows, a bound that some block reaches; each row names 8 different experts. `segments`: in each block of 128 tokens the document ids never fall; each document has 1 to 96 tokens and one has exactly 96.
All inputs are finite; a program needn't handle non-finite values.
Results may differ from the reference program's by a relative error of at most 0.035.
Values may be sent and summed in bfloat16 or wider, within the bound.
No kernel may reach another device: no remote copies, remote signals or barrier semaphores. Data moves between devices by JAX's collectives and lax.ppermute only.
A program may use at most 320 MiB of HBM per device.

```python
import math
import jax
import jax.numpy as jnp
import numpy as np
from jax import lax

D = 2048
HEADS = 16
HD = 128
FF = 1024
NE = 32
TOPK = 8
SEQ_TOK = 128
MICRO = 1
DOCS = 4
DOC_MAX = 96
CAP = 40
TM = 512
N_SECTION = 2
N_EXPERT = 4


def block_levels(stream_key, shape, pieces, low, high):
    def one(dim, blocks):
        heights = jax.random.uniform(jax.random.fold_in(jax.random.fold_in(stream_key, 6), dim), (blocks,), jnp.float32, low / len(pieces), high / len(pieces))
        return jnp.repeat(jnp.exp(heights), shape[dim] // blocks).reshape((-1,) + (1,) * (len(shape) - dim - 1))

    level = one(*pieces[0])
    for cut in pieces[1:]:
        level = level * one(*cut)
    return level


def profile(count, total, reach, skew):
    loads = [(1 << 20) // math.isqrt(grade ** skew) + 1 for grade in range(2, count + 1)]
    surplus, counts = total - reach - (count - 1), [1] * (count - 1)
    while surplus > 0:
        movable = [i for i in range(count - 1) if counts[i] < reach]
        whole, remaining = sum([loads[i] for i in movable]), surplus
        for i in movable:
            more = min(reach - counts[i], max(1, remaining * loads[i] // whole), surplus)
            counts[i] = counts[i] + more
            surplus = surplus - more
    return np.array([reach] + counts)


def uneven_parts(rng, amount, total, most, skew):
    if amount == 2:
        one = jax.random.randint(rng, (), max(1, total - most), min(most, total - 1) + 1)
        return jnp.stack([one, total - one])
    sizes = jnp.asarray(profile(amount, total, most, skew), jnp.int32)
    couples = (amount - 1) // 2
    donor, taker = sizes[1:1 + 2 * couples:2], sizes[2:2 + 2 * couples:2]
    slack = jnp.minimum(donor - 1, most - taker)
    shifted = jax.random.randint(jax.random.fold_in(rng, 1), (couples,), 0, 1 << 20) % (slack + 1)
    sizes = sizes.at[1:1 + 2 * couples:2].set(donor - shifted).at[2:2 + 2 * couples:2].set(taker + shifted)
    return sizes[jax.random.permutation(jax.random.fold_in(rng, 2), amount)]


def shared_out(own_key, own, number, rows, amount, top, most, slope):
    sequence = jax.random.permutation(own_key, amount)
    crowded, usual = portions_of(amount, rows * top, most, slope, True), portions_of(amount, rows * top, most, slope, False)
    places = jnp.arange(amount)

    def named(sizes, rotation):
        used = int((sizes > 0).sum())
        fixed = max(1, used // 4)
        shifted = fixed + (places - fixed + rotation * (used - fixed)) % max(1, amount - fixed)
        return jnp.zeros((amount,), jnp.int32).at[sequence[jnp.where(places < fixed, places, shifted)]].set(jnp.asarray(sizes, jnp.int32))

    sizes = jnp.where(number % 4 == 0, named(crowded, number // 4), named(usual, number - number // 4 - 1))
    mixed = jax.random.permutation(jax.random.fold_in(own, 3), amount)
    source_of, receiver = mixed[0:amount // 2 * 2:2], mixed[1:amount // 2 * 2:2]
    room = jnp.minimum(sizes[source_of] - 1, most - sizes[receiver]) // 2
    room = jnp.where((source_of == sequence[0]) | (receiver == sequence[0]) | (sizes[receiver] == 0), 0, jnp.maximum(room, 0))
    shifted = jax.random.randint(jax.random.fold_in(own, 4), (amount // 2,), 0, 1 << 20) % (room + 1)
    sizes = sizes.at[source_of].add(-shifted).at[receiver].add(shifted)
    items = jnp.searchsorted(jnp.cumsum(sizes), jnp.arange(rows * top), side="right").astype(jnp.int32)
    listing = items.reshape(top, rows).T
    listing = listing[jax.random.permutation(jax.random.fold_in(own, 1), rows)]
    rotation = jax.random.randint(jax.random.fold_in(own, 2), (rows, 1), 0, top)
    return jnp.take_along_axis(listing, (jnp.arange(top)[None, :] + rotation) % top, axis=1)


def portions_of(amount, total, most, skew, full):
    loads = [(1 << 20) // math.isqrt(standing ** skew) + 1 for standing in range(1, amount + 1)]
    largest = most if full else min(most, max(-(-total // amount), total * loads[0] // sum(loads)))
    least = 1 if total - largest >= amount - 1 else 0
    given, spare = [largest] + [least] * (amount - 1), total - largest - least * (amount - 1)
    while spare > 0:
        free = [i for i in range(1, amount) if given[i] < largest] or [i for i in range(1, amount) if given[i] < most]
        whole, budget = sum([loads[i] for i in free]), spare
        for i in free:
            addition = min(most - given[i], max(1, budget * loads[i] // whole), spare)
            given[i] = given[i] + addition
            spare = spare - addition
    return np.array(given)


def gaussian(stream_key, dims, spread, most, split=(), kind=jnp.bfloat16):
    values = jax.random.normal(stream_key, dims, jnp.float32) * spread
    if len(split) > 0:
        values = block_levels(stream_key, dims, split, -0.22, 0.18) * values
    return jnp.clip(values, min=-most, max=most).astype(kind)


def setup_inputs(seed: int = 0) -> dict:
    streams_of = jax.random.split(jax.random.key(seed), 14)
    x_in = gaussian(streams_of[0], (MICRO, TM, D), 1.0, 6.0, ((1, 4),))
    cotangent = gaussian(streams_of[1], (MICRO, TM, D), 1.0, 6.0, ((1, 4),))
    segments = jax.vmap(lambda own: jnp.searchsorted(jnp.cumsum(uneven_parts(own, DOCS, SEQ_TOK, DOC_MAX, 1)), jnp.arange(SEQ_TOK), side="right"))(jax.random.split(streams_of[2], MICRO * N_EXPERT)).reshape((MICRO, N_EXPERT, SEQ_TOK)).astype(jnp.int32)
    routes_keys = jax.random.split(jax.random.fold_in(streams_of[3], 1), N_SECTION * MICRO * TM // SEQ_TOK)
    routes_turns = jax.random.permutation(jax.random.fold_in(streams_of[3], 3), N_SECTION * MICRO * TM // SEQ_TOK)
    routes = jax.vmap(lambda own, number: shared_out(jax.random.fold_in(streams_of[3], 2), own, number, SEQ_TOK, NE, TOPK, CAP, 2))(routes_keys, routes_turns).reshape((N_SECTION, MICRO, TM, TOPK))
    norm1_gain = jnp.clip(1.0 + 0.18 * jax.random.normal(streams_of[4], (N_SECTION, D), jnp.float32), 0.1, 1.9)
    norm2_gain = jnp.clip(1.0 + 0.18 * jax.random.normal(streams_of[5], (N_SECTION, D), jnp.float32), 0.1, 1.9)
    q_gain = jnp.clip(1.0 + 0.18 * jax.random.normal(streams_of[6], (N_SECTION, HD), jnp.float32), 0.1, 1.9)
    k_gain = jnp.clip(1.0 + 0.18 * jax.random.normal(streams_of[7], (N_SECTION, HD), jnp.float32), 0.1, 1.9)
    w_qkv = gaussian(streams_of[8], (N_SECTION, 3, D, HEADS * HD), D ** -0.5, 0.125, ((0, 2), (3, 4)))
    w_o = gaussian(streams_of[9], (N_SECTION, HEADS * HD, D), (HEADS * HD // 32) ** -0.5, 0.75, ((0, 2), (1, 4)))
    router = jnp.clip(jax.random.uniform(streams_of[10], (N_SECTION, D, NE), jnp.float32, -0.019897461, 0.019897461) * block_levels(streams_of[10], (N_SECTION, D, NE), ((0, 2), (1, 4)), -0.4, 0.0), -0.019897461, 0.019897461).astype(jnp.bfloat16)
    w_in = gaussian(streams_of[11], (N_SECTION, NE, D, 2, FF), D ** -0.5, 0.125, ((0, 2), (1, 4), (4, 4)))
    w_out = gaussian(streams_of[12], (N_SECTION, NE, FF, D), (FF // 16) ** -0.5, 0.75, ((0, 2), (1, 4), (2, 4)))
    return {"x_in": x_in, "cotangent": cotangent, "segments": segments, "routes": routes, "norm1_gain": norm1_gain, "norm2_gain": norm2_gain, "q_gain": q_gain, "k_gain": k_gain, "w_qkv": w_qkv, "w_o": w_o, "router": router, "w_in": w_in, "w_out": w_out}


NORM_EPSILON = 1e-06
ROPE_BASE = 10000.0
WIDE_TYPE = jnp.float32
NARROW_TYPE = jnp.bfloat16

def to_narrow(values):
    return lax.optimization_barrier(values.astype(NARROW_TYPE))

def rms_scale(values, gain):
    return values * lax.rsqrt(lax.optimization_barrier(jnp.mean(values * values, axis=-1, keepdims=True)) + NORM_EPSILON) * gain

def block_layout(segment_row, head_dim):
    length = segment_row.shape[0]
    places = jnp.arange(length, dtype=jnp.int32)
    starts = jnp.concatenate([jnp.ones((1,), jnp.int32), (segment_row[1:] != segment_row[:-1]).astype(jnp.int32)])
    first_place = lax.cummax(jnp.where(starts > 0, places, 0), axis=0)
    offsets = (places - first_place).astype(WIDE_TYPE)
    frequency = ROPE_BASE ** (-2.0 * jnp.arange(head_dim // 2, dtype=WIDE_TYPE) / head_dim)
    angles = offsets[:, None] * frequency[None, :]
    allowed = (segment_row[:, None] == segment_row[None, :]) & (places[:, None] >= places[None, :])
    return (jnp.cos(angles), jnp.sin(angles), allowed)

def rotate(tensor, cosine_table, sine_table, direction):
    half_width = tensor.shape[-1] // 2
    first_half = tensor[..., :half_width]
    second_half = tensor[..., half_width:]
    cos_part = cosine_table[:, None, :]
    sin_part = direction * sine_table[:, None, :]
    return jnp.concatenate([first_half * cos_part - second_half * sin_part, second_half * cos_part + first_half * sin_part], axis=-1)

def attend(query_rot, keys_rot, values_head, allowed):
    scale_factor = query_rot.shape[-1] ** (-0.5)
    scores = jnp.einsum('qhd,khd->hqk', query_rot.astype(WIDE_TYPE), keys_rot.astype(WIDE_TYPE)) * scale_factor
    weights = jnp.where(allowed[None], jnp.exp(scores), 0.0)
    totals = lax.optimization_barrier(jnp.sum(weights, axis=-1, keepdims=True))
    attn_probs = to_narrow(weights / totals)
    attended = to_narrow(jnp.einsum('hqk,khd->qhd', attn_probs.astype(WIDE_TYPE), values_head.astype(WIDE_TYPE)))
    return (attended, jnp.log(totals))

def attend_back(query_rot, keys_rot, values_head, attended, log_total, grad_att, allowed):
    scale_factor = query_rot.shape[-1] ** (-0.5)
    scores = jnp.einsum('qhd,khd->hqk', query_rot.astype(WIDE_TYPE), keys_rot.astype(WIDE_TYPE)) * scale_factor
    attn_probs = jnp.where(allowed[None], jnp.exp(scores - log_total), 0.0)
    grad_values = jnp.einsum('hqk,qhd->khd', to_narrow(attn_probs).astype(WIDE_TYPE), grad_att.astype(WIDE_TYPE))
    grad_probs = jnp.einsum('qhd,khd->hqk', grad_att.astype(WIDE_TYPE), values_head.astype(WIDE_TYPE))
    delta_rows = lax.optimization_barrier(jnp.sum(grad_att.astype(WIDE_TYPE) * attended.astype(WIDE_TYPE), axis=-1))
    grad_scores = to_narrow(attn_probs * (grad_probs - jnp.transpose(delta_rows)[:, :, None]))
    grad_query = jnp.einsum('hqk,khd->qhd', grad_scores.astype(WIDE_TYPE), keys_rot.astype(WIDE_TYPE)) * scale_factor
    grad_keys = jnp.einsum('hqk,qhd->khd', grad_scores.astype(WIDE_TYPE), query_rot.astype(WIDE_TYPE)) * scale_factor
    return (grad_query, grad_keys, grad_values)

def attention_pieces(block_in, segment_row, gain_one, gain_query, gain_key, qkv_wide):
    token_count = block_in.shape[0]
    cosine_table, sine_table, allowed = block_layout(segment_row, HD)
    normed_one = to_narrow(rms_scale(block_in.astype(WIDE_TYPE), gain_one))
    projected = jnp.einsum('sd,ide->ise', normed_one.astype(WIDE_TYPE), qkv_wide)
    query_raw = projected[0].reshape(token_count, HEADS, HD)
    keys_raw = projected[1].reshape(token_count, HEADS, HD)
    values_head = to_narrow(projected[2].reshape(token_count, HEADS, HD))
    query_rot = to_narrow(rotate(rms_scale(query_raw, gain_query), cosine_table, sine_table, 1.0))
    keys_rot = to_narrow(rotate(rms_scale(keys_raw, gain_key), cosine_table, sine_table, 1.0))
    attended, log_total = attend(query_rot, keys_rot, values_head, allowed)
    return (cosine_table, sine_table, allowed, normed_one, query_raw, keys_raw, values_head, query_rot, keys_rot, attended, log_total)

def middle_rows(blocks_in, segment_blocks, layer_params):
    gain_one, gain_two, gain_query, gain_key, qkv_weight, out_weight, router_weight, in_weight, out_experts = layer_params
    qkv_wide = qkv_weight.astype(WIDE_TYPE)

    def one_block(block_pair):
        block_in, segment_row = block_pair
        attended = attention_pieces(block_in, segment_row, gain_one, gain_query, gain_key, qkv_wide)[9]
        joined = attended.reshape(block_in.shape[0], HEADS * HD)
        return block_in.astype(WIDE_TYPE) + jnp.dot(joined, out_weight, preferred_element_type=WIDE_TYPE)
    return lax.map(one_block, (blocks_in, segment_blocks)).reshape(-1, D)

def routing_of(middle, route_flat, gain_two, router_weight):
    normed_two = to_narrow(rms_scale(middle, gain_two))
    logits = jnp.dot(normed_two, router_weight, preferred_element_type=WIDE_TYPE)
    logit_exps = jnp.exp(logits)
    route_probs = logit_exps / lax.optimization_barrier(jnp.sum(logit_exps, axis=-1, keepdims=True))
    chosen = route_flat[:, :, None] == jnp.arange(NE, dtype=jnp.int32)[None, None, :]
    gate_weights = lax.optimization_barrier(jnp.sum(jnp.where(chosen, route_probs[:, None, :], 0.0), axis=-1))
    block_count = route_flat.shape[0] // SEQ_TOK
    per_block = route_flat.reshape(block_count, SEQ_TOK * TOPK)
    onehot = (per_block[:, :, None] == jnp.arange(NE, dtype=jnp.int32)[None, None, :]).astype(jnp.int32)
    before = jnp.cumsum(onehot, axis=1) - onehot
    slot_rank = lax.optimization_barrier(jnp.sum(before * onehot, axis=-1))
    block_ids = jnp.arange(block_count, dtype=jnp.int32)[:, None]
    slot_place = ((per_block * block_count + block_ids) * CAP + slot_rank).reshape(-1).astype(jnp.int32)
    slot_total = NE * block_count * CAP
    slot_owner = jnp.zeros((slot_total,), jnp.int32).at[slot_place].set(jnp.arange(slot_place.shape[0], dtype=jnp.int32))
    filled = jnp.zeros((slot_total,), WIDE_TYPE).at[slot_place].set(1.0)
    return (normed_two, route_probs, gate_weights, chosen, slot_place, slot_owner, filled)

def expert_rows(row_data, weight_in, weight_out):
    gate_proj = jnp.dot(row_data, weight_in[:, 0, :], preferred_element_type=WIDE_TYPE)
    up_proj = jnp.dot(row_data, weight_in[:, 1, :], preferred_element_type=WIDE_TYPE)
    silu_gate = gate_proj * jax.nn.sigmoid(gate_proj)
    hidden = to_narrow(silu_gate * up_proj)
    out_rows = jnp.dot(hidden, weight_out, preferred_element_type=WIDE_TYPE)
    return (gate_proj, up_proj, silu_gate, hidden, out_rows)

def mixture_forward(routing, in_weight, out_experts):
    normed_two, route_probs, gate_weights, chosen, slot_place, slot_owner, filled = routing
    rows_each = slot_owner.shape[0] // NE
    owners = slot_owner.reshape(NE, rows_each)
    gate_slots = (gate_weights.reshape(-1)[slot_owner] * filled).reshape(NE, rows_each)

    def expert_step(cumulative_accum, inputs):
        weight_in, weight_out, owner_row, gate_row = inputs
        token_ids = owner_row // TOPK
        out_rows = expert_rows(normed_two[token_ids], weight_in, weight_out)[4]
        return (cumulative_accum.at[token_ids].add(gate_row[:, None] * out_rows), None)
    mixed_out, _ = lax.scan(expert_step, jnp.zeros((normed_two.shape[0], D), WIDE_TYPE), (in_weight, out_experts, owners, gate_slots))
    return mixed_out

def layer_forward(blocks_in, segment_blocks, route_flat, layer_params):
    middle = middle_rows(blocks_in, segment_blocks, layer_params)
    routing = routing_of(middle, route_flat, layer_params[1], layer_params[6])
    mixed_out = mixture_forward(routing, layer_params[7], layer_params[8])
    return to_narrow(middle + mixed_out).reshape(blocks_in.shape)

def layer_backward(blocks_in, segment_blocks, route_flat, layer_params, grad_blocks):
    gain_one, gain_two, gain_query, gain_key, qkv_weight, out_weight, router_weight, in_weight, out_experts = layer_params
    middle = middle_rows(blocks_in, segment_blocks, layer_params)
    normed_two, route_probs, gate_weights, chosen, slot_place, slot_owner, filled = routing_of(middle, route_flat, gain_two, router_weight)
    grad_out = grad_blocks.reshape(-1, D).astype(WIDE_TYPE)
    rows_each = slot_owner.shape[0] // NE
    owners = slot_owner.reshape(NE, rows_each)
    fills = filled.reshape(NE, rows_each)
    gate_slots = (gate_weights.reshape(-1)[slot_owner] * filled).reshape(NE, rows_each)

    def expert_step(cumulative_accum, inputs):
        weight_in, weight_out, owner_row, gate_row, fill_row = inputs
        token_ids = owner_row // TOPK
        row_data = normed_two[token_ids]
        gate_proj, up_proj, silu_gate, hidden, out_rows = expert_rows(row_data, weight_in, weight_out)
        upstream = grad_out[token_ids]
        slot_grad = lax.optimization_barrier(jnp.sum(upstream * out_rows, axis=-1)) * fill_row
        grad_rows = to_narrow(gate_row[:, None] * upstream)
        grad_hidden = jnp.dot(grad_rows, weight_out.T, preferred_element_type=WIDE_TYPE)
        grad_wout = jnp.dot(hidden.T, grad_rows, preferred_element_type=WIDE_TYPE)
        sigmoid_gate = jax.nn.sigmoid(gate_proj)
        grad_gate = to_narrow(grad_hidden * up_proj * sigmoid_gate * (1.0 + gate_proj * (1.0 - sigmoid_gate)))
        grad_up = to_narrow(grad_hidden * silu_gate)
        grad_win = jnp.stack([jnp.dot(row_data.T, grad_gate, preferred_element_type=WIDE_TYPE), jnp.dot(row_data.T, grad_up, preferred_element_type=WIDE_TYPE)], axis=1)
        grad_in_rows = jnp.dot(grad_gate, weight_in[:, 0, :].T, preferred_element_type=WIDE_TYPE) + jnp.dot(grad_up, weight_in[:, 1, :].T, preferred_element_type=WIDE_TYPE)
        return (cumulative_accum.at[token_ids].add(grad_in_rows), (slot_grad, grad_win, grad_wout))
    grad_norm, (slot_grads, grad_win, grad_wout) = lax.scan(expert_step, jnp.zeros((normed_two.shape[0], D), WIDE_TYPE), (in_weight, out_experts, owners, gate_slots, fills))
    gate_grads = slot_grads.reshape(-1)[slot_place].reshape(-1, TOPK)
    grad_probs = lax.optimization_barrier(jnp.sum(jnp.where(chosen, gate_grads[:, :, None], 0.0), axis=1))
    grad_logit = route_probs * (grad_probs - lax.optimization_barrier(jnp.sum(route_probs * grad_probs, axis=-1, keepdims=True)))
    grad_norm = grad_norm + jnp.dot(grad_logit, router_weight.astype(WIDE_TYPE).T, precision=lax.Precision.HIGHEST)
    router_grad = jnp.dot(normed_two.astype(WIDE_TYPE).T, grad_logit, precision=lax.Precision.HIGHEST)
    _, pull_two = jax.vjp(rms_scale, middle, gain_two)
    grad_mid_norm, gain_two_grad = pull_two(grad_norm)
    grad_middle = (grad_out + grad_mid_norm).reshape(blocks_in.shape)
    qkv_wide = qkv_weight.astype(WIDE_TYPE)

    def attn_step(cumulative_accum, inputs):
        block_in, segment_row, grad_mid_block = inputs
        token_count = block_in.shape[0]
        cosine_table, sine_table, allowed, normed_one, query_raw, keys_raw, values_head, query_rot, keys_rot, attended, log_total = attention_pieces(block_in, segment_row, gain_one, gain_query, gain_key, qkv_wide)
        grad_mid_narrow = to_narrow(grad_mid_block)
        grad_att = to_narrow(jnp.dot(grad_mid_narrow, out_weight.T, preferred_element_type=WIDE_TYPE)).reshape(token_count, HEADS, HD)
        exit_matrix_slope = jnp.dot(attended.reshape(token_count, -1).T, grad_mid_narrow, preferred_element_type=WIDE_TYPE)
        grad_qrot, grad_krot, grad_values = attend_back(query_rot, keys_rot, values_head, attended, log_total, grad_att, allowed)
        _, pull_query = jax.vjp(rms_scale, query_raw, gain_query)
        grad_query, probe_scale_slope = pull_query(rotate(grad_qrot, cosine_table, sine_table, -1.0))
        _, pull_key = jax.vjp(rms_scale, keys_raw, gain_key)
        grad_keys, lookup_scale_slope = pull_key(rotate(grad_krot, cosine_table, sine_table, -1.0))
        grad_proj = to_narrow(jnp.stack([grad_query, grad_keys, grad_values]).reshape(3, token_count, HEADS * HD))
        attention_matrix_slope = jnp.einsum('sd,ise->ide', normed_one.astype(WIDE_TYPE), grad_proj.astype(WIDE_TYPE))
        grad_norm_one = jnp.einsum('ise,ide->sd', grad_proj.astype(WIDE_TYPE), qkv_wide)
        _, pull_one = jax.vjp(rms_scale, block_in.astype(WIDE_TYPE), gain_one)
        grad_x_norm, norm_one_scale_slope = pull_one(grad_norm_one)
        incoming_slope = to_narrow(grad_mid_block + grad_x_norm)
        summand_list = (attention_matrix_slope, exit_matrix_slope, norm_one_scale_slope, probe_scale_slope, lookup_scale_slope)
        return (jax.tree.map(lambda former_factor, latter_factor: former_factor + latter_factor, cumulative_accum, summand_list), incoming_slope)
    start_sums = (jnp.zeros((3, D, HEADS * HD), WIDE_TYPE), jnp.zeros((HEADS * HD, D), WIDE_TYPE), jnp.zeros((D,), WIDE_TYPE), jnp.zeros((HD,), WIDE_TYPE), jnp.zeros((HD,), WIDE_TYPE))
    (qkv_sum, wo_sum, g1_sum, gq_sum, gk_sum), grad_inputs = lax.scan(attn_step, start_sums, (blocks_in, segment_blocks, grad_middle))
    return (grad_inputs, g1_sum, gain_two_grad, gq_sum, gk_sum, qkv_sum, wo_sum, router_grad, grad_win, grad_wout)

def reference(x_in, cotangent, segments, routes, norm1_gain, norm2_gain, q_gain, k_gain, w_qkv, w_o, router, w_in, w_out):
    block_count = MICRO * N_EXPERT
    segment_blocks = segments.reshape(block_count, SEQ_TOK)
    section_inputs = []
    layer_outputs = []
    current = x_in.reshape(block_count, SEQ_TOK, D)
    all_params = []
    for layer_index in range(N_SECTION):
        layer_params = (norm1_gain[layer_index], norm2_gain[layer_index], q_gain[layer_index], k_gain[layer_index], w_qkv[layer_index], w_o[layer_index], router[layer_index], w_in[layer_index], w_out[layer_index])
        all_params.append(layer_params)
        section_inputs.append(current)
        current = layer_forward(current, segment_blocks, routes[layer_index].reshape(-1, TOPK), layer_params)
        layer_outputs.append(current)
    grad_current = cotangent.reshape(block_count, SEQ_TOK, D)
    results = [None] * N_SECTION
    for layer_index in reversed(range(N_SECTION)):
        results[layer_index] = layer_backward(section_inputs[layer_index], segment_blocks, routes[layer_index].reshape(-1, TOPK), all_params[layer_index], grad_current)
        grad_current = results[layer_index][0]
    out_shape = (N_SECTION, MICRO, N_EXPERT * SEQ_TOK, D)
    layer_out = jnp.stack(layer_outputs).reshape(out_shape)
    input_grad = jnp.stack([entry[0] for entry in results]).reshape(out_shape)
    stacked = [jnp.stack([entry[position] for entry in results]) for position in range(1, 10)]
    return (layer_out, input_grad, stacked[0], stacked[1], stacked[2], stacked[3], stacked[4], stacked[5], stacked[6], stacked[7], stacked[8])
```

```python
import jax
import jax.numpy as jnp
from jax import lax
from jax.sharding import PartitionSpec as P


NORM_EPSILON = 1e-06
ROPE_BASE = 10000.0
F32 = jnp.float32
BF16 = jnp.bfloat16
AXES = ("section", "expert", "head")


def device_pairs(source_section, target_section, expert_shift, head_flip):
    expert_count = lax.axis_size("expert")
    head_count = lax.axis_size("head")

    def place(section, expert, head):
        return (section * expert_count + expert) * head_count + head

    return [
        (
            place(source_section, e, h),
            place(target_section, (e - expert_shift) % expert_count, h ^ head_flip),
        )
        for e in range(expert_count)
        for h in range(head_count)
    ]


def move(array, source_section, target_section, expert_shift=0, head_flip=0):
    return lax.ppermute(
        array, AXES, device_pairs(source_section, target_section, expert_shift, head_flip)
    )


def head_sum(partial, section):
    narrow = lax.optimization_barrier(partial.astype(BF16))
    parts = [narrow] + [
        move(narrow, section, section, head_flip=d) for d in range(1, lax.axis_size("head"))
    ]
    parts = [part.astype(F32) for part in parts]
    while len(parts) > 1:
        parts = [parts[i] + parts[i + 1] for i in range(0, len(parts), 2)]
    return parts[0]


def group_rows(own, section):
    return [own] + [
        move(own, section, section, expert_shift=r) for r in range(1, lax.axis_size("expert"))
    ]


def group_sum(blocks, section):
    total = blocks[0].astype(F32)
    for r in range(1, len(blocks)):
        total = total + move(blocks[r], section, section, expert_shift=-r).astype(F32)
    return total


def rms_scale(values, gain):
    return (
        values * lax.rsqrt(jnp.mean(values * values, axis=-1, keepdims=True) + NORM_EPSILON) * gain
    )


def block_layout(segment_row, head_dim):
    length = segment_row.shape[0]
    places = jnp.arange(length, dtype=jnp.int32)
    allowed = (segment_row[:, None] == segment_row[None, :]) & (places[:, None] >= places[None, :])
    offsets = jnp.sum(allowed.astype(F32), axis=1) - 1.0
    frequency = ROPE_BASE ** (-2.0 * jnp.arange(head_dim // 2, dtype=F32) / head_dim)
    angles = offsets[:, None] * frequency[None, :]
    return (jnp.cos(angles), jnp.sin(angles), allowed)


def rotate(tensor, cosine_table, sine_table, direction):
    half_width = tensor.shape[-1] // 2
    first_half = tensor[..., :half_width]
    second_half = tensor[..., half_width:]
    cos_part = cosine_table[:, None, :]
    sin_part = direction * sine_table[:, None, :]
    return jnp.concatenate(
        [
            first_half * cos_part - second_half * sin_part,
            second_half * cos_part + first_half * sin_part,
        ],
        axis=-1,
    )


def attend(query_rot, keys_rot, values_head, allowed):
    scale_factor = query_rot.shape[-1] ** (-0.5)
    scores = (
        jnp.einsum("qhd,khd->hqk", query_rot, keys_rot, preferred_element_type=F32) * scale_factor
    )
    weights = jnp.where(allowed[None], jnp.exp(scores), 0.0)
    totals = jnp.sum(weights, axis=-1, keepdims=True)
    attn_probs = (weights / totals).astype(BF16)
    attended = jnp.einsum(
        "hqk,khd->qhd", attn_probs, values_head, preferred_element_type=F32
    ).astype(BF16)
    return (attended, jnp.log(totals))


def attend_back(query_rot, keys_rot, values_head, attended, log_total, grad_att, allowed):
    scale_factor = query_rot.shape[-1] ** (-0.5)
    scores = (
        jnp.einsum("qhd,khd->hqk", query_rot, keys_rot, preferred_element_type=F32) * scale_factor
    )
    attn_probs = jnp.where(allowed[None], jnp.exp(scores - log_total), 0.0)
    grad_values = jnp.einsum(
        "hqk,qhd->khd", attn_probs.astype(BF16), grad_att, preferred_element_type=F32
    )
    grad_probs = jnp.einsum("qhd,khd->hqk", grad_att, values_head, preferred_element_type=F32)
    delta_rows = jnp.sum(grad_att.astype(F32) * attended.astype(F32), axis=-1)
    grad_scores = (attn_probs * (grad_probs - jnp.transpose(delta_rows)[:, :, None])).astype(BF16)
    grad_query = (
        jnp.einsum("hqk,khd->qhd", grad_scores, keys_rot, preferred_element_type=F32)
        * scale_factor
    )
    grad_keys = (
        jnp.einsum("hqk,qhd->khd", grad_scores, query_rot, preferred_element_type=F32)
        * scale_factor
    )
    return (grad_query, grad_keys, grad_values)


def attention_forward(layer_in, tables, weights):
    cosine_table, sine_table, allowed = tables
    token_count = layer_in.shape[0]
    head_dim = weights["q_gain"].shape[0]
    normed = rms_scale(layer_in.astype(F32), weights["gain_one"]).astype(BF16)
    projected = jnp.einsum("sd,ide->ise", normed, weights["w_qkv"], preferred_element_type=F32)
    query_raw = projected[0].reshape(token_count, -1, head_dim)
    keys_raw = projected[1].reshape(token_count, -1, head_dim)
    values_head = projected[2].reshape(token_count, -1, head_dim).astype(BF16)
    query_rot = rotate(
        rms_scale(query_raw, weights["q_gain"]), cosine_table, sine_table, 1.0
    ).astype(BF16)
    keys_rot = rotate(
        rms_scale(keys_raw, weights["k_gain"]), cosine_table, sine_table, 1.0
    ).astype(BF16)
    attended, log_total = attend(query_rot, keys_rot, values_head, allowed)
    partial = jnp.dot(
        attended.reshape(token_count, -1), weights["w_o"], preferred_element_type=F32
    )
    saved = (normed, query_raw, keys_raw, values_head, query_rot, keys_rot, attended, log_total)
    return partial, saved


def attention_backward(grad_middle, saved, tables, weights):
    normed, query_raw, keys_raw, values_head, query_rot, keys_rot, attended, log_total = saved
    cosine_table, sine_table, allowed = tables
    token_count = grad_middle.shape[0]
    head_dim = weights["q_gain"].shape[0]
    grad_narrow = grad_middle.astype(BF16)
    grad_att = (
        jnp.dot(grad_narrow, weights["w_o"].T, preferred_element_type=F32)
        .astype(BF16)
        .reshape(token_count, -1, head_dim)
    )
    grad_qrot, grad_krot, grad_values = attend_back(
        query_rot, keys_rot, values_head, attended, log_total, grad_att, allowed
    )
    _, pull_query = jax.vjp(rms_scale, query_raw, weights["q_gain"])
    grad_query, query_gain_grad = pull_query(rotate(grad_qrot, cosine_table, sine_table, -1.0))
    _, pull_key = jax.vjp(rms_scale, keys_raw, weights["k_gain"])
    grad_keys, key_gain_grad = pull_key(rotate(grad_krot, cosine_table, sine_table, -1.0))
    grad_proj = (
        jnp.stack([grad_query, grad_keys, grad_values]).reshape(3, token_count, -1).astype(BF16)
    )
    partial = jnp.einsum("ise,ide->sd", grad_proj, weights["w_qkv"], preferred_element_type=F32)
    return partial, grad_narrow, grad_proj, query_gain_grad, key_gain_grad


def route_probabilities(rows, router):
    logits = jnp.dot(rows, router, preferred_element_type=F32)
    logit_exps = jnp.exp(logits)
    return logit_exps / jnp.sum(logit_exps, axis=-1, keepdims=True)


def expert_forward(rows, gates, weights):
    joined = jnp.einsum("td,edjf->tejf", rows, weights["w_in"], preferred_element_type=F32)
    gate_proj = joined[:, :, 0, :]
    up_proj = joined[:, :, 1, :]
    hidden = gate_proj * jax.nn.sigmoid(gate_proj) * up_proj
    weighted = (hidden * gates[:, :, None]).astype(BF16)
    partial = jnp.einsum("tef,efd->td", weighted, weights["w_out"], preferred_element_type=F32)
    return partial.astype(BF16), joined, weighted


def expert_backward(grad_rows, gates, joined, weights):
    gate_proj = joined[:, :, 0, :]
    up_proj = joined[:, :, 1, :]
    grad_raw = jnp.einsum("td,efd->tef", grad_rows, weights["w_out"], preferred_element_type=F32)
    sigmoid_gate = jax.nn.sigmoid(gate_proj)
    silu_gate = gate_proj * sigmoid_gate
    hidden = (silu_gate * up_proj).astype(BF16).astype(F32)
    gate_grads = jnp.sum(hidden * grad_raw, axis=-1)
    grad_hidden = grad_raw * gates[:, :, None]
    grad_gate = (
        grad_hidden * up_proj * sigmoid_gate * (1.0 + gate_proj * (1.0 - sigmoid_gate))
    ).astype(BF16)
    grad_up = (grad_hidden * silu_gate).astype(BF16)
    grad_joined = jnp.stack([grad_gate, grad_up], axis=2)
    partial = jnp.einsum("tejf,edjf->td", grad_joined, weights["w_in"], preferred_element_type=F32)
    return partial.astype(BF16), gate_grads, grad_joined


def body(
    x_in,
    cotangent,
    segments,
    routes,
    norm1_gain,
    norm2_gain,
    q_gain,
    k_gain,
    w_qkv,
    w_o,
    router,
    w_in,
    w_out,
):
    section_index = lax.axis_index("section")
    expert_index = lax.axis_index("expert")
    head_index = lax.axis_index("head")
    groups = lax.axis_size("expert")
    first_section = 0
    last_section = lax.axis_size("section") - 1
    on_first = section_index == first_section
    layer_start = x_in[0]
    token_count, model_width = layer_start.shape
    head_dim = q_gain.shape[1]
    expert_count = router.shape[2]
    local_experts = w_in.shape[1]
    width_part = norm1_gain.shape[1]

    gains = lax.all_gather(jnp.concatenate([norm1_gain, norm2_gain]), "head", axis=1, tiled=True)
    router_full = lax.all_gather(router[0], "head", axis=0, tiled=True)
    weights = {
        "gain_one": gains[0],
        "gain_two": gains[1],
        "q_gain": q_gain[0],
        "k_gain": k_gain[0],
        "w_qkv": w_qkv[0],
        "w_o": w_o[0],
        "w_in": w_in[0],
        "w_out": w_out[0],
    }
    tables = block_layout(segments[0, 0], head_dim)

    def rolled(gathered):
        doubled = jnp.concatenate([gathered, gathered])
        return lax.dynamic_slice_in_dim(
            doubled, expert_index * token_count, groups * token_count, 0
        )

    routes_all = rolled(lax.all_gather(routes[0, 0], "expert", axis=0, tiled=True))
    columns = jnp.arange(expert_count, dtype=jnp.int32)
    chosen_all = jnp.any(routes_all[:, :, None] == columns[None, None, :], axis=1)
    own_columns = columns // local_experts == expert_index
    cotangent_all = rolled(lax.all_gather(cotangent[0], "expert", axis=0, tiled=True))

    def layer_forward(layer_in, section, earlier):
        partial, saved = attention_forward(layer_in, tables, weights)
        attention_sum = head_sum(partial, section)
        if earlier is not None:
            attention_sum = jnp.where(on_first, earlier[0], attention_sum)
        middle = layer_in.astype(F32) + attention_sum
        normed = rms_scale(middle, weights["gain_two"]).astype(BF16)
        blocks = group_rows(normed, section)
        rows = jnp.concatenate(blocks)
        if earlier is not None:
            rows = jnp.where(on_first, earlier[1], rows)
        probs = route_probabilities(rows, router_full)
        gates = lax.dynamic_slice_in_dim(
            jnp.where(chosen_all, probs, 0.0), expert_index * local_experts, local_experts, 1
        )
        mixed, joined, weighted = expert_forward(rows, gates, weights)
        mixed = group_sum(jnp.split(mixed, groups), section)
        result = (middle + head_sum(mixed, section)).astype(BF16)
        if earlier is not None:
            result = jnp.where(on_first, earlier[2], result)
        kept = (middle, normed, rows, probs[:token_count], gates, joined, weighted)
        return (attention_sum, rows, result), saved, kept

    def layer_backward(grad_all, saved, kept, layer_in, section, earlier):
        middle, normed, rows, probs, gates, joined, weighted = kept
        partial, gate_grads, grad_joined = expert_backward(grad_all, gates, joined, weights)
        placed = jnp.where(
            own_columns[None, :], jnp.tile(gate_grads, (1, groups)), 0.0
        ).astype(BF16)
        lane_pad = -expert_count % 128
        placed = jnp.pad(placed, ((0, 0), (0, lane_pad)))
        joined_grads = jnp.concatenate([partial, placed], axis=1)
        total = head_sum(group_sum(jnp.split(joined_grads, groups), section), section)
        if earlier is not None:
            total = jnp.where(on_first, total, earlier[0])
        upstream = grad_all[:token_count].astype(F32)
        grad_probs = jnp.where(
            chosen_all[:token_count], total[:, model_width : model_width + expert_count], 0.0
        )
        grad_logit = probs * (grad_probs - jnp.sum(probs * grad_probs, axis=-1, keepdims=True))
        grad_norm = total[:, :model_width] + jnp.dot(
            grad_logit, router_full.astype(F32).T, precision=lax.Precision.HIGHEST
        )
        _, pull_two = jax.vjp(rms_scale, middle, weights["gain_two"])
        grad_mid_norm, gain_two_grad = pull_two(grad_norm)
        grad_middle = upstream + grad_mid_norm
        partial_one, grad_narrow, grad_proj, query_gain_grad, key_gain_grad = attention_backward(
            grad_middle, saved, tables, weights
        )
        total_one = head_sum(partial_one, section)
        if earlier is not None:
            total_one = jnp.where(on_first, total_one, earlier[1])
        wide_in = layer_in.astype(F32)
        _, pull_one = jax.vjp(rms_scale, wide_in, weights["gain_one"])
        grad_x_norm, _ = pull_one(total_one)
        result = (grad_middle + grad_x_norm).astype(BF16)
        own_norm = wide_in * lax.rsqrt(
            jnp.mean(wide_in * wide_in, axis=-1, keepdims=True) + NORM_EPSILON
        )
        gain_one_part = jnp.sum(partial_one * own_norm, axis=0)
        terms = (
            grad_joined,
            grad_logit,
            gain_two_grad,
            gain_one_part,
            grad_narrow,
            grad_proj,
            query_gain_grad,
            key_gain_grad,
        )
        return (total, total_one), result, terms

    exchanged, _, _ = layer_forward(layer_start, first_section, None)
    arrived = move(exchanged[2], first_section, last_section)
    layer_in = jnp.where(on_first, layer_start, arrived)
    exchanged, saved, kept = layer_forward(layer_in, last_section, exchanged)
    layer_result = exchanged[2]

    exchanged, grad_result, _ = layer_backward(
        cotangent_all, saved, kept, layer_in, last_section, None
    )
    arrived_all = jnp.concatenate(
        [move(grad_result, last_section, first_section, expert_shift=r) for r in range(groups)]
    )
    grad_all = jnp.where(on_first, arrived_all, cotangent_all)
    _, grad_result, terms = layer_backward(
        grad_all, saved, kept, layer_in, first_section, exchanged
    )
    (
        grad_joined,
        grad_logit,
        gain_two_grad,
        gain_one_part,
        grad_narrow,
        grad_proj,
        query_gain_grad,
        key_gain_grad,
    ) = terms
    normed_one, attended = saved[0], saved[6].reshape(token_count, -1)
    normed_two, rows, weighted = kept[1], kept[2], kept[6]

    grad_w_out = jnp.einsum("tef,td->efd", weighted, grad_all, preferred_element_type=F32)
    grad_w_in = jnp.einsum("td,tejf->edjf", rows, grad_joined, preferred_element_type=F32)

    def own_width(array, axis):
        return lax.dynamic_slice_in_dim(array, head_index * width_part, width_part, axis)

    router_part = jnp.dot(
        own_width(normed_two, 1).astype(F32).T, grad_logit, precision=lax.Precision.HIGHEST
    )
    router_own, gain_two_own = lax.psum((router_part, own_width(gain_two_grad, 0)), "expert")
    gain_one_sum, query_gain_sum, key_gain_sum = lax.psum(
        (gain_one_part, query_gain_grad, key_gain_grad), ("expert", "head")
    )
    gain_one_own = own_width(gain_one_sum, 0)

    slab = model_width // groups

    def own_slab(array):
        gathered = lax.all_gather(array, "expert", axis=0, tiled=True)
        return lax.dynamic_slice_in_dim(gathered, expert_index * slab, slab, 1)

    attended_all = lax.all_gather(attended, "expert", axis=0, tiled=True)
    grad_w_o = jnp.einsum(
        "te,td->ed", attended_all, own_slab(grad_narrow), preferred_element_type=F32
    )
    grad_proj_all = lax.all_gather(grad_proj, "expert", axis=1, tiled=True)
    grad_w_qkv = jnp.einsum(
        "td,ite->ide", own_slab(normed_one), grad_proj_all, preferred_element_type=F32
    )
    return (
        layer_result[None, None],
        grad_result[None, None],
        gain_one_own[None],
        gain_two_own[None],
        query_gain_sum[None],
        key_gain_sum[None],
        grad_w_qkv[None],
        grad_w_o[None],
        router_own[None],
        grad_w_in[None],
        grad_w_out[None],
    )


def solution(mesh):
    placed = (
        P(None, "expert", None),
        P(None, "expert", None),
        P(None, "expert", None),
        P("section", None, "expert", None),
        P("section", "head"),
        P("section", "head"),
        P("section", None),
        P("section", None),
        P("section", None, None, "head"),
        P("section", "head", None),
        P("section", "head", None),
        P("section", "expert", None, None, "head"),
        P("section", "expert", "head", None),
    )
    return jax.shard_map(
        body,
        mesh=mesh,
        in_specs=placed,
        out_specs=(
            P("section", None, "expert", None),
            P("section", None, "expert", None),
            P("section", "head"),
            P("section", "head"),
            P("section", None),
            P("section", None),
            P("section", None, "expert", "head"),
            P("section", "head", "expert"),
            P("section", "head", None),
            P("section", "expert", None, None, "head"),
            P("section", "expert", "head", None),
        ),
        check_vma=False,
    )
```

```python
import jax
import jax.numpy as jnp
from jax import lax
from jax.experimental import pallas as pl
from jax.experimental.pallas import tpu as pltpu
from jax.sharding import PartitionSpec as P


NORM_EPSILON = 1e-06
ROPE_BASE = 10000.0
F32 = jnp.float32
BF16 = jnp.bfloat16
AXES = ("section", "expert", "head")


def device_pairs(source_section, target_section, expert_shift, head_flip):
    expert_count = lax.axis_size("expert")
    head_count = lax.axis_size("head")

    def place(section, expert, head):
        return (section * expert_count + expert) * head_count + head

    return [
        (
            place(source_section, e, h),
            place(target_section, (e - expert_shift) % expert_count, h ^ head_flip),
        )
        for e in range(expert_count)
        for h in range(head_count)
    ]


def move(array, source_section, target_section, expert_shift=0, head_flip=0):
    return lax.ppermute(
        array, AXES, device_pairs(source_section, target_section, expert_shift, head_flip)
    )


def spread(blocks):
    pairs_of = lambda r: sum(
        (device_pairs(s, s, -r, 0) for s in range(lax.axis_size("section"))), []
    )
    return [blocks[0]] + [
        lax.ppermute(blocks[r], AXES, pairs_of(r)) for r in range(1, len(blocks))
    ]


def spread_section(blocks, section):
    return [blocks[0]] + [
        move(blocks[r], section, section, expert_shift=-r) for r in range(1, len(blocks))
    ]


def split_pair(values):
    high = lax.reduce_precision(values, 8, 7)
    return high, values - high


def head_sum(partial, section):
    narrow = lax.optimization_barrier(partial.astype(BF16))
    parts = [narrow] + [
        move(narrow, section, section, head_flip=d) for d in range(1, lax.axis_size("head"))
    ]
    parts = [part.astype(F32) for part in parts]
    while len(parts) > 1:
        parts = [parts[i] + parts[i + 1] for i in range(0, len(parts), 2)]
    return parts[0]


def group_rows(own, section):
    return [own] + [
        move(own, section, section, expert_shift=r) for r in range(1, lax.axis_size("expert"))
    ]


def group_sum(blocks, section):
    total = blocks[0].astype(F32)
    for r in range(1, len(blocks)):
        total = total + move(blocks[r], section, section, expert_shift=-r).astype(F32)
    return total


def rms_scale(values, gain):
    return (
        values * lax.rsqrt(jnp.mean(values * values, axis=-1, keepdims=True) + NORM_EPSILON) * gain
    )


def block_layout(segment_row, head_dim):
    length = segment_row.shape[0]
    places = jnp.arange(length, dtype=jnp.int32)
    allowed = (segment_row[:, None] == segment_row[None, :]) & (places[:, None] >= places[None, :])
    offsets = jnp.sum(allowed.astype(F32), axis=1) - 1.0
    frequency = ROPE_BASE ** (-2.0 * jnp.arange(head_dim // 2, dtype=F32) / head_dim)
    angles = offsets[:, None] * frequency[None, :]
    cosine, sine = jnp.cos(angles), jnp.sin(angles)
    return (
        jnp.concatenate([cosine, cosine], axis=1),
        jnp.concatenate([-sine, sine], axis=1),
        allowed.astype(F32),
    )


def turned(values, cosine, sine):
    return values * cosine + pltpu.roll(values, values.shape[-1] // 2, 1) * sine


def attention_kernel(
    proj_ref, q_gain_ref, k_gain_ref, cos_ref, sin_ref, mask_ref, rq_ref, rk_ref, vh_ref, att_ref
):
    scale_factor = cos_ref.shape[1] ** (-0.5)
    cosine, sine = cos_ref[...], sin_ref[...]
    query = turned(rms_scale(proj_ref[0], q_gain_ref[...]), cosine, sine).astype(BF16)
    keys = turned(rms_scale(proj_ref[1], k_gain_ref[...]), cosine, sine).astype(BF16)
    values = proj_ref[2].astype(BF16)
    scores = (
        lax.dot_general(query, keys, (((1,), (1,)), ((), ())), preferred_element_type=F32)
        * scale_factor
    )
    weights = jnp.where(mask_ref[...] > 0, jnp.exp(scores), 0.0)
    probs = (weights / jnp.sum(weights, axis=-1, keepdims=True)).astype(BF16)
    att_ref[...] = jnp.dot(probs, values, preferred_element_type=F32).astype(BF16)
    rq_ref[...] = query
    rk_ref[...] = keys
    vh_ref[...] = values


def attention_back_kernel(
    proj_ref,
    q_gain_ref,
    k_gain_ref,
    cos_ref,
    sin_ref,
    mask_ref,
    rq_ref,
    rk_ref,
    vh_ref,
    att_ref,
    grad_ref,
    out_ref,
    q_grad_ref,
    k_grad_ref,
):
    scale_factor = cos_ref.shape[1] ** (-0.5)
    cosine, sine = cos_ref[...], sin_ref[...]
    query, keys, values, grad_att = rq_ref[...], rk_ref[...], vh_ref[...], grad_ref[...]
    scores = (
        lax.dot_general(query, keys, (((1,), (1,)), ((), ())), preferred_element_type=F32)
        * scale_factor
    )
    weights = jnp.where(mask_ref[...] > 0, jnp.exp(scores), 0.0)
    probs = weights / jnp.sum(weights, axis=-1, keepdims=True)
    grad_values = lax.dot_general(
        probs.astype(BF16), grad_att, (((0,), (0,)), ((), ())), preferred_element_type=F32
    )
    grad_probs = lax.dot_general(
        grad_att, values, (((1,), (1,)), ((), ())), preferred_element_type=F32
    )
    delta = jnp.sum(
        grad_att.astype(F32) * att_ref[...].astype(F32), axis=-1, keepdims=True
    )
    grad_scores = (probs * (grad_probs - delta)).astype(BF16)
    grad_query = jnp.dot(grad_scores, keys, preferred_element_type=F32) * scale_factor
    grad_keys = (
        lax.dot_general(
            grad_scores, query, (((0,), (0,)), ((), ())), preferred_element_type=F32
        )
        * scale_factor
    )

    def back(raw, gain, grad):
        grad_normed = turned(grad, cosine, -sine)
        inverse = lax.rsqrt(jnp.mean(raw * raw, axis=-1, keepdims=True) + NORM_EPSILON)
        normed = raw * inverse
        gained = grad_normed * gain
        grad_raw = inverse * (gained - normed * jnp.mean(gained * normed, axis=-1, keepdims=True))
        return grad_raw, jnp.sum(grad_normed * normed, axis=0, keepdims=True)

    grad_raw_query, q_grad = back(proj_ref[0], q_gain_ref[...], grad_query)
    grad_raw_keys, k_grad = back(proj_ref[1], k_gain_ref[...], grad_keys)
    out_ref[0] = grad_raw_query.astype(BF16)
    out_ref[1] = grad_raw_keys.astype(BF16)
    out_ref[2] = grad_values.astype(BF16)

    @pl.when(pl.program_id(0) == 0)
    def _():
        q_grad_ref[...] = jnp.zeros_like(q_grad_ref)
        k_grad_ref[...] = jnp.zeros_like(k_grad_ref)

    q_grad_ref[...] += q_grad
    k_grad_ref[...] += k_grad


def head_specs(token_count, head_dim):
    def whole(*shape):
        return pl.BlockSpec(shape, lambda h: (0, 0))

    column = pl.BlockSpec((token_count, head_dim), lambda h: (0, h))
    triple = pl.BlockSpec((3, token_count, head_dim), lambda h: (0, 0, h))
    shared = [
        triple,
        whole(1, head_dim),
        whole(1, head_dim),
        whole(token_count, head_dim),
        whole(token_count, head_dim),
        whole(token_count, token_count),
    ]
    return whole(1, head_dim), column, triple, shared


def attend(projected, tables, weights):
    _, token_count, width = projected.shape
    head_dim = weights["q_gain"].shape[1]
    _, column, _, shared = head_specs(token_count, head_dim)
    rows = jax.ShapeDtypeStruct((token_count, width), BF16)
    return pl.pallas_call(
        attention_kernel,
        out_shape=(rows,) * 4,
        grid=(width // head_dim,),
        in_specs=shared,
        out_specs=[column] * 4,
        name="attention",
    )(projected, weights["q_gain"], weights["k_gain"], *tables)


def attend_back(projected, tables, weights, rotated, grad_att):
    _, token_count, width = projected.shape
    head_dim = weights["q_gain"].shape[1]
    gain, column, triple, shared = head_specs(token_count, head_dim)
    return pl.pallas_call(
        attention_back_kernel,
        out_shape=(
            jax.ShapeDtypeStruct(projected.shape, BF16),
            jax.ShapeDtypeStruct((1, head_dim), F32),
            jax.ShapeDtypeStruct((1, head_dim), F32),
        ),
        grid=(width // head_dim,),
        in_specs=shared + [column] * 5,
        out_specs=[triple, gain, gain],
        name="attention_back",
    )(projected, weights["q_gain"], weights["k_gain"], *tables, *rotated, grad_att)


def weight_kernel(rows_ref, grads_ref, weighted_ref, upstream_ref, in_ref, out_ref):
    width = rows_ref.shape[0]
    parts = grads_ref.shape[3] // 128
    for j in range(2):
        product = jnp.dot(rows_ref[...], grads_ref[0, j], preferred_element_type=F32)
        for c in range(parts):
            in_ref[0, pl.ds(2 * c + j, width, stride=2 * parts), :] = product[
                :, 128 * c : 128 * (c + 1)
            ]
    out_ref[0] = lax.dot_general(
        weighted_ref[0], upstream_ref[...], (((0,), (0,)), ((), ())), preferred_element_type=F32
    )


def weight_grads(rows_turned, grad_joined, weighted, upstream):
    width, token_count = rows_turned.shape
    experts, _, _, hidden = grad_joined.shape
    flat = 2 * hidden // 128 * width
    grad_in, grad_out = pl.pallas_call(
        weight_kernel,
        out_shape=(
            jax.ShapeDtypeStruct((experts, flat, 128), F32),
            jax.ShapeDtypeStruct((experts, hidden, width), F32),
        ),
        grid=(experts,),
        in_specs=[
            pl.BlockSpec((width, token_count), lambda e: (0, 0)),
            pl.BlockSpec((1, 2, token_count, hidden), lambda e: (e, 0, 0, 0)),
            pl.BlockSpec((1, token_count, hidden), lambda e: (e, 0, 0)),
            pl.BlockSpec((token_count, width), lambda e: (0, 0)),
        ],
        out_specs=[
            pl.BlockSpec((1, flat, 128), lambda e: (e, 0, 0)),
            pl.BlockSpec((1, hidden, width), lambda e: (e, 0, 0)),
        ],
        compiler_params=pltpu.CompilerParams(vmem_limit_bytes=56 << 20),
        name="weight_grads",
    )(rows_turned, grad_joined, weighted, upstream)
    grad_in = grad_in.reshape(experts, width, hidden // 128, 2, 128)
    return jnp.swapaxes(grad_in, 2, 3).reshape(experts, width, 2, hidden), grad_out


def attention_forward(layer_in, tables, weights):
    normed = rms_scale(layer_in.astype(F32), weights["gain_one"]).astype(BF16)
    projected = jnp.einsum("sd,ide->ise", normed, weights["w_qkv"], preferred_element_type=F32)
    rotated = attend(projected, tables, weights)
    partial = jnp.dot(rotated[3], weights["w_o"], preferred_element_type=F32)
    return partial, (normed, projected, rotated)


def route_probabilities(rows, router):
    logits = jnp.dot(rows, router, preferred_element_type=F32)
    logit_exps = jnp.exp(logits)
    return logit_exps / jnp.sum(logit_exps, axis=-1, keepdims=True)


def gated(gate_proj, up_proj):
    sigmoid_gate = 0.5 * jnp.tanh(0.5 * gate_proj) + 0.5
    silu_gate = gate_proj * sigmoid_gate
    return sigmoid_gate, silu_gate, silu_gate * up_proj


def own_gates(rows_ref, pick_ref, width):
    packed = rows_ref[:, width:].astype(F32)
    return jnp.sum(packed * pick_ref[0], axis=1, keepdims=True)


def dot_turned(left, right):
    return lax.dot_general(left, right, (((1,), (1,)), ((), ())), preferred_element_type=F32)


def clear_first(*refs):
    @pl.when(pl.program_id(1) == 0)
    def _():
        for ref in refs:
            ref[...] = jnp.zeros_like(ref)


def join_weights(in_ref, join_ref):
    hidden = in_ref.shape[3]
    join_ref[:, :hidden] = in_ref[0, 0]
    join_ref[:, hidden:] = in_ref[1, 0]


def expert_forward_kernel(rows_ref, pick_ref, in_ref, out_ref, partial_ref, acc_ref):
    width = out_ref.shape[2]
    clear_first(acc_ref)
    rows = rows_ref[:, :width]
    gate_proj = jnp.dot(rows, in_ref[0, 0], preferred_element_type=F32)
    up_proj = jnp.dot(rows, in_ref[1, 0], preferred_element_type=F32)
    _, _, hidden = gated(gate_proj, up_proj)
    weighted = (hidden * own_gates(rows_ref, pick_ref, width)).astype(BF16)
    acc_ref[...] += jnp.dot(weighted, out_ref[0], preferred_element_type=F32)

    @pl.when(pl.program_id(1) == pl.num_programs(1) - 1)
    def _():
        partial_ref[...] = acc_ref[...].astype(BF16)


def expert_grads(
    gate_proj, up_proj, gates, upstream, join_ref, out_ref, acc_ref, gate_acc_ref, place
):
    sigmoid_gate, silu_gate, hidden = gated(gate_proj, up_proj)
    grad_raw = dot_turned(upstream, out_ref[0])
    gate_acc_ref[...] += jnp.sum(hidden * grad_raw, axis=1, keepdims=True) * place
    grad_hidden = grad_raw * gates
    grad_gate = (
        grad_hidden * up_proj * sigmoid_gate * (1.0 + gate_proj * (1.0 - sigmoid_gate))
    ).astype(BF16)
    grad_up = (grad_hidden * silu_gate).astype(BF16)
    acc_ref[...] += dot_turned(jnp.concatenate([grad_gate, grad_up], axis=1), join_ref[...])
    return grad_gate, grad_up, (hidden * gates).astype(BF16)


def store_last(partial_ref, acc_ref, gate_acc_ref):
    @pl.when(pl.program_id(1) == pl.num_programs(1) - 1)
    def _():
        width = acc_ref.shape[1]
        partial_ref[:, :width] = acc_ref[...].astype(BF16)
        partial_ref[:, width:] = gate_acc_ref[...].astype(BF16)


def expert_both_kernel(
    rows_ref,
    upstream_ref,
    pick_ref,
    place_ref,
    in_ref,
    out_ref,
    joined_ref,
    weighted_ref,
    partial_ref,
    acc_ref,
    gate_acc_ref,
    join_ref,
):
    width = out_ref.shape[2]
    hidden = out_ref.shape[1]
    join_weights(in_ref, join_ref)
    clear_first(acc_ref, gate_acc_ref)
    both = jnp.dot(rows_ref[:, :width], join_ref[...], preferred_element_type=F32)
    gate_proj, up_proj = both[:, :hidden], both[:, hidden:]
    joined_ref[0, 0] = gate_proj.astype(BF16)
    joined_ref[0, 1] = up_proj.astype(BF16)
    gates = own_gates(rows_ref, pick_ref, width)
    _, _, weighted_ref[0] = expert_grads(
        gate_proj,
        up_proj,
        gates,
        upstream_ref[...],
        join_ref,
        out_ref,
        acc_ref,
        gate_acc_ref,
        place_ref[0],
    )
    store_last(partial_ref, acc_ref, gate_acc_ref)


def expert_back_kernel(
    rows_ref,
    upstream_ref,
    pick_ref,
    place_ref,
    in_ref,
    out_ref,
    joined_ref,
    grads_ref,
    partial_ref,
    acc_ref,
    gate_acc_ref,
    join_ref,
):
    width = out_ref.shape[2]
    hidden = out_ref.shape[1]
    join_weights(in_ref, join_ref)
    clear_first(acc_ref, gate_acc_ref)
    gates = own_gates(rows_ref, pick_ref, width)
    grads_ref[0, 0], grads_ref[0, 1], _ = expert_grads(
        joined_ref[0, 0].astype(F32),
        joined_ref[0, 1].astype(F32),
        gates,
        upstream_ref[...],
        join_ref,
        out_ref,
        acc_ref,
        gate_acc_ref,
        place_ref[0],
    )
    store_last(partial_ref, acc_ref, gate_acc_ref)


def expert_call(kernel, name, rows, upstream, weights, extra_in=(), outs=(), grads=True):
    w_in, w_out = weights["w_in"], weights["w_out"]
    _, experts, width, hidden = w_in.shape
    token_count, total = rows.shape
    extra = total - width
    block = min(token_count, 512)

    def per_expert(*lead):
        zeros = (0,) * len(lead)
        return (
            jax.ShapeDtypeStruct((experts,) + lead + (token_count, hidden), BF16),
            pl.BlockSpec((1,) + lead + (block, hidden), lambda t, e: (e,) + zeros + (t, 0)),
        )

    def row_block(columns):
        return pl.BlockSpec((block, columns), lambda t, e: (t, 0))

    lane = pl.BlockSpec((1, 1, extra), lambda t, e: (e, 0, 0))
    out_width = total if grads else width
    outputs = [per_expert(*lead) for lead in outs] + [
        (jax.ShapeDtypeStruct((token_count, out_width), BF16), row_block(out_width))
    ]
    first = [rows] + ([upstream] if grads else [])
    marks = [weights["pick"]] + ([weights["place"]] if grads else [])
    return pl.pallas_call(
        kernel,
        out_shape=[shape for shape, _ in outputs],
        grid=(token_count // block, experts),
        in_specs=[row_block(array.shape[1]) for array in first]
        + [lane] * len(marks)
        + [
            pl.BlockSpec((2, 1, width, hidden), lambda t, e: (0, e, 0, 0)),
            pl.BlockSpec((1, hidden, width), lambda t, e: (e, 0, 0)),
        ]
        + [per_expert(2)[1] for _ in extra_in],
        out_specs=[spec for _, spec in outputs],
        scratch_shapes=[pltpu.VMEM((block, width), F32)]
        + (
            [pltpu.VMEM((block, extra), F32), pltpu.VMEM((width, 2 * hidden), BF16)]
            if grads
            else []
        ),
        compiler_params=pltpu.CompilerParams(vmem_limit_bytes=60 << 20),
        name=name,
    )(*first, *marks, w_in, w_out, *extra_in)


def body(
    x_in,
    cotangent,
    segments,
    routes,
    norm1_gain,
    norm2_gain,
    q_gain,
    k_gain,
    w_qkv,
    w_o,
    router,
    w_in,
    w_out,
):
    section_index = lax.axis_index("section")
    expert_index = lax.axis_index("expert")
    head_index = lax.axis_index("head")
    groups = lax.axis_size("expert")
    first_section = 0
    last_section = lax.axis_size("section") - 1
    on_first = section_index == first_section
    layer_start = x_in[0]
    token_count, model_width = layer_start.shape
    head_dim = q_gain.shape[1]
    expert_count = router.shape[2]
    local_experts = w_in.shape[1]
    width_part = norm1_gain.shape[1]
    head_width = w_o.shape[1]
    lane_pad = -expert_count % 64
    extra = 2 * (expert_count + lane_pad)

    shared = jnp.concatenate(
        [norm1_gain, norm2_gain, router[0].astype(F32).T], axis=0
    )
    shared = lax.all_gather(shared, "head", axis=1, tiled=True)
    router_wide = shared[2:].T
    router_full = router_wide.astype(BF16)
    weights = {
        "gain_one": shared[0],
        "gain_two": shared[1],
        "q_gain": q_gain,
        "k_gain": k_gain,
        "w_qkv": w_qkv[0],
        "w_o": w_o[0],
        "w_out": w_out[0],
    }
    tables = block_layout(segments[0, 0], head_dim)
    columns = jnp.arange(expert_count, dtype=jnp.int32)
    chosen = jnp.any(routes[0, 0][:, :, None] == columns[None, None, :], axis=1)
    lanes = jnp.arange(extra, dtype=jnp.int32)[None, None, :]
    own_experts = expert_index * local_experts + jnp.arange(local_experts, dtype=jnp.int32)
    weights["pick"] = (lanes % (extra // 2) == own_experts[:, None, None]).astype(F32)
    weights["place"] = (lanes == own_experts[:, None, None]).astype(F32)

    slab = model_width // groups

    def slabs(array):
        return [
            lax.dynamic_slice_in_dim(array, (expert_index + r) % groups * slab, slab, 1)
            for r in range(groups)
        ]

    def early_blocks(saved):
        return [jnp.concatenate([block, saved[2][3]], axis=1) for block in slabs(saved[0])]

    def layer_forward(layer_in, section, earlier, beside=None):
        partial, saved = attention_forward(layer_in, tables, weights)
        if beside is not None:
            partial, beside = lax.optimization_barrier((partial, beside))
        attention_sum = head_sum(partial, section)
        if earlier is not None:
            beside = spread_section(early_blocks(saved), first_section)
            attention_sum, beside = lax.optimization_barrier((attention_sum, beside))
            attention_sum = jnp.where(on_first, earlier[0], attention_sum)
        middle = layer_in.astype(F32) + attention_sum
        normed = rms_scale(middle, weights["gain_two"]).astype(BF16)
        probs = route_probabilities(normed, router_full)
        high, low = split_pair(jnp.where(chosen, probs, 0.0))
        pad = jnp.zeros((token_count, lane_pad), F32)
        sent = jnp.concatenate(
            [normed] + [part.astype(BF16) for part in (high, pad, low, pad)], axis=1
        )
        if earlier is None:
            sent, own_in = lax.optimization_barrier((sent, w_in[0]))
            weights["w_in"] = jnp.transpose(own_in, (2, 0, 1, 3))
        rows = jnp.concatenate(group_rows(sent, section))
        if earlier is not None:
            rows = jnp.where(on_first, earlier[1], rows)
        return (attention_sum, rows), saved, (middle, normed, probs), beside

    def layer_output(middle, mixed, section):
        mixed = group_sum(jnp.split(mixed, groups), section)
        return (middle + head_sum(mixed, section)).astype(BF16)

    def own_width(array, axis):
        return lax.dynamic_slice_in_dim(array, head_index * width_part, width_part, axis)

    def layer_backward(partial, experts, grad_all, saved, kept, layer_in, section, earlier):
        normed_one, projected, rotated = saved
        middle, normed, probs = kept
        summed = group_sum(jnp.split(partial, groups), section)
        expert_sums = None
        if earlier is None:
            summed, expert_sums = lax.optimization_barrier((summed, experts))
        else:
            expert_sums = weight_grads(*experts, grad_all)
            first_blocks, later_blocks = earlier[2]
            summed, expert_sums, later_blocks = lax.optimization_barrier(
                (summed, expert_sums, later_blocks)
            )
            later_blocks = spread_section(later_blocks, last_section)
        total = head_sum(summed, section)
        if earlier is not None:
            total = jnp.where(on_first, total, earlier[0])
        upstream = grad_all[:token_count].astype(F32)
        grad_probs = jnp.where(chosen, total[:, model_width : model_width + expert_count], 0.0)
        grad_logit = probs * (grad_probs - jnp.sum(probs * grad_probs, axis=-1, keepdims=True))
        grad_norm = total[:, :model_width] + jnp.dot(
            grad_logit, router_wide.T, precision=lax.Precision.HIGHEST
        )
        _, pull_two = jax.vjp(rms_scale, middle, weights["gain_two"])
        grad_mid_norm, gain_two_grad = pull_two(grad_norm)
        grad_middle = upstream + grad_mid_norm
        grad_narrow = grad_middle.astype(BF16)
        router_part = jnp.dot(
            grad_logit.T, own_width(normed, 1).astype(F32), precision=lax.Precision.HIGHEST
        )
        router_part = jnp.concatenate([router_part, own_width(gain_two_grad, 0)[None]])
        if earlier is not None:
            grad_narrow, router_part = lax.optimization_barrier((grad_narrow, router_part))
        grad_att = lax.dot_general(
            grad_narrow, weights["w_o"], (((1,), (1,)), ((), ())), preferred_element_type=F32
        ).astype(BF16)
        grad_proj, q_grad, k_grad = attend_back(projected, tables, weights, rotated, grad_att)
        wide_proj = jnp.concatenate(list(grad_proj), axis=1)
        grad_blocks = [jnp.concatenate([block, wide_proj], axis=1) for block in slabs(grad_narrow)]
        if earlier is not None:
            grad_blocks = spread_section(grad_blocks, section)
        partial_one = jnp.einsum(
            "ise,ide->sd", grad_proj, weights["w_qkv"], preferred_element_type=F32
        )
        wide_in = layer_in.astype(F32)
        own_norm = wide_in * lax.rsqrt(
            jnp.mean(wide_in * wide_in, axis=-1, keepdims=True) + NORM_EPSILON
        )
        gain_one_part = jnp.sum(partial_one * own_norm, axis=0, keepdims=True)
        gain_pair = jnp.concatenate([q_grad, k_grad], axis=1)
        gain_pair = jnp.pad(gain_pair, ((0, 0), (0, model_width - 2 * head_dim)))
        tail_rows = split_pair(gain_one_part) + split_pair(gain_pair)
        tail_rows = jnp.pad(jnp.concatenate(tail_rows), ((0, 16 - len(tail_rows)), (0, 0)))
        total_one = head_sum(jnp.concatenate([partial_one, tail_rows]), section)
        if earlier is not None:
            total_one = jnp.where(on_first, total_one, earlier[1])
            grad_blocks = [
                jnp.where(on_first, jnp.concatenate([a, b], axis=1), c)
                for a, b, c in zip(grad_blocks, first_blocks, later_blocks)
            ]
        _, pull_one = jax.vjp(rms_scale, wide_in, weights["gain_one"])
        grad_x_norm, _ = pull_one(total_one[:token_count])
        result = (grad_middle + grad_x_norm).astype(BF16)
        return (total, total_one, grad_blocks), result, router_part, expert_sums

    cotangent_all = jnp.concatenate(group_rows(cotangent[0], last_section))
    exchanged, _, kept, cotangent_all = layer_forward(
        layer_start, first_section, None, cotangent_all
    )
    (mixed,) = expert_call(
        expert_forward_kernel, "experts", exchanged[1], None, weights, grads=False
    )
    first_result = layer_output(kept[0], mixed, first_section)
    arrived = move(first_result, first_section, last_section)
    layer_in = jnp.where(on_first, layer_start, arrived)
    exchanged, saved, kept, first_blocks = layer_forward(layer_in, last_section, exchanged)
    rows = exchanged[1]
    joined, weighted, partial = expert_call(
        expert_both_kernel,
        "experts_both",
        rows,
        cotangent_all,
        weights,
        outs=((2,), ()),
    )
    mixed = jnp.einsum(
        "etf,efd->td", weighted, weights["w_out"], preferred_element_type=F32
    ).astype(BF16)
    exchanged, grad_result, _, (rows_turned, mixed) = layer_backward(
        partial, (rows[:, :model_width].T, mixed), cotangent_all, saved, kept, layer_in, last_section, None
    )
    later = [
        jnp.concatenate([a, b], axis=1) for a, b in zip(exchanged[2], early_blocks(saved))
    ]
    exchanged = exchanged[:2] + ((first_blocks, later),)
    arrived_all = jnp.concatenate(
        [move(grad_result, last_section, first_section, expert_shift=r) for r in range(groups)]
    )
    mixed, arrived_all = lax.optimization_barrier((mixed, arrived_all))
    last_result = layer_output(kept[0], mixed, last_section)
    layer_result = jnp.where(on_first, first_result, last_result)
    grad_all = jnp.where(on_first, arrived_all, cotangent_all)
    grad_joined, partial = expert_call(
        expert_back_kernel,
        "experts_back",
        rows,
        grad_all,
        weights,
        extra_in=(joined,),
        outs=((2,),),
    )
    exchanged, grad_result, router_part, (grad_w_in, grad_w_out) = layer_backward(
        partial,
        (rows_turned, grad_joined, weighted),
        grad_all,
        saved,
        kept,
        layer_in,
        first_section,
        exchanged,
    )

    tail_rows = exchanged[1][token_count:]
    gains_own = jnp.concatenate(
        [
            own_width(tail_rows[0] + tail_rows[1], 0),
            (tail_rows[2] + tail_rows[3])[: 2 * head_dim],
            router_part.reshape(-1),
        ]
    ).reshape(-1, 128)
    grad_blocks, _ = lax.optimization_barrier((exchanged[2], gains_own))
    gains_parts = jnp.stack(spread([gains_own] * groups))
    gains_order = (expert_index - jnp.arange(groups, dtype=jnp.int32)) % groups
    gains_sum = jnp.sum(gains_parts[gains_order], axis=0).reshape(-1)
    router_sum = gains_sum[width_part + 2 * head_dim :].reshape(expert_count + 1, width_part)
    grad_rows = jnp.concatenate(grad_blocks)
    proj_end = slab + 3 * head_width
    slab_rows = grad_rows[:, proj_end : proj_end + slab]
    attended_rows = grad_rows[:, proj_end + slab :]
    grad_w_o = jnp.einsum(
        "te,td->ed", attended_rows, grad_rows[:, :slab], preferred_element_type=F32
    )
    grad_w_qkv = jnp.stack(
        [
            jnp.einsum("td,te->de", slab_rows, part, preferred_element_type=F32)
            for part in jnp.split(grad_rows[:, slab:proj_end], 3, axis=1)
        ]
    )
    return (
        layer_result[None, None],
        grad_result[None, None],
        gains_sum[None, :width_part],
        router_sum[expert_count:],
        gains_sum[None, width_part : width_part + head_dim],
        gains_sum[None, width_part + head_dim : width_part + 2 * head_dim],
        grad_w_qkv[None],
        grad_w_o[None],
        router_sum[:expert_count].T[None],
        grad_w_in[None],
        grad_w_out[None],
    )


def solution(mesh):
    placed = (
        P(None, "expert", None),
        P(None, "expert", None),
        P(None, "expert", None),
        P("section", None, "expert", None),
        P("section", "head"),
        P("section", "head"),
        P("section", None),
        P("section", None),
        P("section", None, None, "head"),
        P("section", "head", None),
        P("section", "head", None),
        P("section", "expert", None, None, "head"),
        P("section", "expert", "head", None),
    )
    return jax.shard_map(
        body,
        mesh=mesh,
        in_specs=placed,
        out_specs=(
            P("section", None, "expert", None),
            P("section", None, "expert", None),
            P("section", "head"),
            P("section", "head"),
            P("section", None),
            P("section", None),
            P("section", None, "expert", "head"),
            P("section", "head", "expert"),
            P("section", "head", None),
            P("section", "expert", None, None, "head"),
            P("section", "expert", "head", None),
        ),
        check_vma=False,
    )
```

```python
import jax
import jax.numpy as jnp
from jax import lax
from jax.experimental import pallas as pl
from jax.experimental.pallas import tpu as pltpu
from jax.sharding import PartitionSpec as P


NORM_EPSILON = 1e-06
ROPE_BASE = 10000.0
F32 = jnp.float32
BF16 = jnp.bfloat16
AXES = ("section", "expert", "head")


def device_pairs(source_section, target_section, expert_shift, head_flip):
    expert_count = lax.axis_size("expert")
    head_count = lax.axis_size("head")

    def place(section, expert, head):
        return (section * expert_count + expert) * head_count + head

    return [
        (
            place(source_section, e, h),
            place(target_section, (e - expert_shift) % expert_count, h ^ head_flip),
        )
        for e in range(expert_count)
        for h in range(head_count)
    ]


def move(array, source_section, target_section, expert_shift=0, head_flip=0):
    return lax.ppermute(
        array, AXES, device_pairs(source_section, target_section, expert_shift, head_flip)
    )


def spread(blocks):
    pairs_of = lambda r: sum(
        (device_pairs(s, s, -r, 0) for s in range(lax.axis_size("section"))), []
    )
    return [blocks[0]] + [
        lax.ppermute(blocks[r], AXES, pairs_of(r)) for r in range(1, len(blocks))
    ]


def spread_section(blocks, section):
    return [blocks[0]] + [
        move(blocks[r], section, section, expert_shift=-r) for r in range(1, len(blocks))
    ]


def split_pair(values):
    high = lax.reduce_precision(values, 8, 7)
    return high, values - high


def head_sum(partial, section):
    narrow = lax.optimization_barrier(partial.astype(BF16))
    parts = [narrow] + [
        move(narrow, section, section, head_flip=d) for d in range(1, lax.axis_size("head"))
    ]
    parts = [part.astype(F32) for part in parts]
    while len(parts) > 1:
        parts = [parts[i] + parts[i + 1] for i in range(0, len(parts), 2)]
    return parts[0]


def group_rows(own, section):
    return [own] + [
        move(own, section, section, expert_shift=r) for r in range(1, lax.axis_size("expert"))
    ]


def group_sum(blocks, section):
    total = blocks[0].astype(F32)
    for r in range(1, len(blocks)):
        total = total + move(blocks[r], section, section, expert_shift=-r).astype(F32)
    return total


def rms_scale(values, gain):
    return (
        values * lax.rsqrt(jnp.mean(values * values, axis=-1, keepdims=True) + NORM_EPSILON) * gain
    )


def block_layout(segment_row, head_dim):
    length = segment_row.shape[0]
    places = jnp.arange(length, dtype=jnp.int32)
    allowed = (segment_row[:, None] == segment_row[None, :]) & (places[:, None] >= places[None, :])
    offsets = jnp.sum(allowed.astype(F32), axis=1) - 1.0
    frequency = ROPE_BASE ** (-2.0 * jnp.arange(head_dim // 2, dtype=F32) / head_dim)
    angles = offsets[:, None] * frequency[None, :]
    cosine, sine = jnp.cos(angles), jnp.sin(angles)
    return (
        jnp.concatenate([cosine, cosine], axis=1),
        jnp.concatenate([-sine, sine], axis=1),
        allowed.astype(F32),
    )


def turned(values, cosine, sine):
    return values * cosine + pltpu.roll(values, values.shape[-1] // 2, 1) * sine


def attention_kernel(
    proj_ref, q_gain_ref, k_gain_ref, cos_ref, sin_ref, mask_ref, rq_ref, rk_ref, vh_ref, att_ref
):
    scale_factor = cos_ref.shape[1] ** (-0.5)
    cosine, sine = cos_ref[...], sin_ref[...]
    query = turned(rms_scale(proj_ref[0], q_gain_ref[...]), cosine, sine).astype(BF16)
    keys = turned(rms_scale(proj_ref[1], k_gain_ref[...]), cosine, sine).astype(BF16)
    values = proj_ref[2].astype(BF16)
    scores = (
        lax.dot_general(query, keys, (((1,), (1,)), ((), ())), preferred_element_type=F32)
        * scale_factor
    )
    weights = jnp.where(mask_ref[...] > 0, jnp.exp(scores), 0.0)
    probs = (weights / jnp.sum(weights, axis=-1, keepdims=True)).astype(BF16)
    att_ref[...] = jnp.dot(probs, values, preferred_element_type=F32).astype(BF16)
    rq_ref[...] = query
    rk_ref[...] = keys
    vh_ref[...] = values


def attention_back_kernel(
    proj_ref,
    q_gain_ref,
    k_gain_ref,
    cos_ref,
    sin_ref,
    mask_ref,
    rq_ref,
    rk_ref,
    vh_ref,
    att_ref,
    grad_ref,
    out_ref,
    q_grad_ref,
    k_grad_ref,
):
    scale_factor = cos_ref.shape[1] ** (-0.5)
    cosine, sine = cos_ref[...], sin_ref[...]
    query, keys, values, grad_att = rq_ref[...], rk_ref[...], vh_ref[...], grad_ref[...]
    scores = (
        lax.dot_general(query, keys, (((1,), (1,)), ((), ())), preferred_element_type=F32)
        * scale_factor
    )
    weights = jnp.where(mask_ref[...] > 0, jnp.exp(scores), 0.0)
    probs = weights / jnp.sum(weights, axis=-1, keepdims=True)
    grad_values = lax.dot_general(
        probs.astype(BF16), grad_att, (((0,), (0,)), ((), ())), preferred_element_type=F32
    )
    grad_probs = lax.dot_general(
        grad_att, values, (((1,), (1,)), ((), ())), preferred_element_type=F32
    )
    delta = jnp.sum(
        grad_att.astype(F32) * att_ref[...].astype(F32), axis=-1, keepdims=True
    )
    grad_scores = (probs * (grad_probs - delta)).astype(BF16)
    grad_query = jnp.dot(grad_scores, keys, preferred_element_type=F32) * scale_factor
    grad_keys = (
        lax.dot_general(
            grad_scores, query, (((0,), (0,)), ((), ())), preferred_element_type=F32
        )
        * scale_factor
    )

    def back(raw, gain, grad):
        grad_normed = turned(grad, cosine, -sine)
        inverse = lax.rsqrt(jnp.mean(raw * raw, axis=-1, keepdims=True) + NORM_EPSILON)
        normed = raw * inverse
        gained = grad_normed * gain
        grad_raw = inverse * (gained - normed * jnp.mean(gained * normed, axis=-1, keepdims=True))
        return grad_raw, jnp.sum(grad_normed * normed, axis=0, keepdims=True)

    grad_raw_query, q_grad = back(proj_ref[0], q_gain_ref[...], grad_query)
    grad_raw_keys, k_grad = back(proj_ref[1], k_gain_ref[...], grad_keys)
    out_ref[0] = grad_raw_query.astype(BF16)
    out_ref[1] = grad_raw_keys.astype(BF16)
    out_ref[2] = grad_values.astype(BF16)

    @pl.when(pl.program_id(0) == 0)
    def _():
        q_grad_ref[...] = jnp.zeros_like(q_grad_ref)
        k_grad_ref[...] = jnp.zeros_like(k_grad_ref)

    q_grad_ref[...] += q_grad
    k_grad_ref[...] += k_grad


def head_specs(token_count, head_dim):
    def whole(*shape):
        return pl.BlockSpec(shape, lambda h: (0, 0))

    column = pl.BlockSpec((token_count, head_dim), lambda h: (0, h))
    triple = pl.BlockSpec((3, token_count, head_dim), lambda h: (0, 0, h))
    shared = [
        triple,
        whole(1, head_dim),
        whole(1, head_dim),
        whole(token_count, head_dim),
        whole(token_count, head_dim),
        whole(token_count, token_count),
    ]
    return whole(1, head_dim), column, triple, shared


def attend(projected, tables, weights):
    _, token_count, width = projected.shape
    head_dim = weights["q_gain"].shape[1]
    _, column, _, shared = head_specs(token_count, head_dim)
    rows = jax.ShapeDtypeStruct((token_count, width), BF16)
    return pl.pallas_call(
        attention_kernel,
        out_shape=(rows,) * 4,
        grid=(width // head_dim,),
        in_specs=shared,
        out_specs=[column] * 4,
        name="attention",
    )(projected, weights["q_gain"], weights["k_gain"], *tables)


def attend_back(projected, tables, weights, rotated, grad_att):
    _, token_count, width = projected.shape
    head_dim = weights["q_gain"].shape[1]
    gain, column, triple, shared = head_specs(token_count, head_dim)
    return pl.pallas_call(
        attention_back_kernel,
        out_shape=(
            jax.ShapeDtypeStruct(projected.shape, BF16),
            jax.ShapeDtypeStruct((1, head_dim), F32),
            jax.ShapeDtypeStruct((1, head_dim), F32),
        ),
        grid=(width // head_dim,),
        in_specs=shared + [column] * 5,
        out_specs=[triple, gain, gain],
        name="attention_back",
    )(projected, weights["q_gain"], weights["k_gain"], *tables, *rotated, grad_att)


def weight_kernel(rows_ref, grads_ref, weighted_ref, upstream_ref, in_ref, out_ref):
    width = rows_ref.shape[0]
    parts = grads_ref.shape[3] // 128
    for j in range(2):
        product = jnp.dot(rows_ref[...], grads_ref[0, j], preferred_element_type=F32)
        for c in range(parts):
            in_ref[0, pl.ds(2 * c + j, width, stride=2 * parts), :] = product[
                :, 128 * c : 128 * (c + 1)
            ]
    out_ref[0] = lax.dot_general(
        weighted_ref[0], upstream_ref[...], (((0,), (0,)), ((), ())), preferred_element_type=F32
    )


def weight_grads(rows_turned, grad_joined, weighted, upstream):
    width, token_count = rows_turned.shape
    experts, _, _, hidden = grad_joined.shape
    flat = 2 * hidden // 128 * width
    grad_in, grad_out = pl.pallas_call(
        weight_kernel,
        out_shape=(
            jax.ShapeDtypeStruct((experts, flat, 128), F32),
            jax.ShapeDtypeStruct((experts, hidden, width), F32),
        ),
        grid=(experts,),
        in_specs=[
            pl.BlockSpec((width, token_count), lambda e: (0, 0)),
            pl.BlockSpec((1, 2, token_count, hidden), lambda e: (e, 0, 0, 0)),
            pl.BlockSpec((1, token_count, hidden), lambda e: (e, 0, 0)),
            pl.BlockSpec((token_count, width), lambda e: (0, 0)),
        ],
        out_specs=[
            pl.BlockSpec((1, flat, 128), lambda e: (e, 0, 0)),
            pl.BlockSpec((1, hidden, width), lambda e: (e, 0, 0)),
        ],
        compiler_params=pltpu.CompilerParams(vmem_limit_bytes=56 << 20),
        name="weight_grads",
    )(rows_turned, grad_joined, weighted, upstream)
    grad_in = grad_in.reshape(experts, width, hidden // 128, 2, 128)
    return jnp.swapaxes(grad_in, 2, 3).reshape(experts, width, 2, hidden), grad_out


def attention_forward(layer_in, tables, weights):
    normed = rms_scale(layer_in.astype(F32), weights["gain_one"]).astype(BF16)
    projected = jnp.einsum("sd,ide->ise", normed, weights["w_qkv"], preferred_element_type=F32)
    rotated = attend(projected, tables, weights)
    partial = jnp.dot(rotated[3], weights["w_o"], preferred_element_type=F32)
    return partial, (normed, projected, rotated)


def route_probabilities(rows, router):
    logits = jnp.dot(rows, router, preferred_element_type=F32)
    logit_exps = jnp.exp(logits)
    return logit_exps / jnp.sum(logit_exps, axis=-1, keepdims=True)


def gated(gate_proj, up_proj):
    sigmoid_gate = 0.5 * jnp.tanh(0.5 * gate_proj) + 0.5
    silu_gate = gate_proj * sigmoid_gate
    return sigmoid_gate, silu_gate, silu_gate * up_proj


def own_gates(rows_ref, pick_ref, width):
    packed = rows_ref[:, width:].astype(F32)
    return jnp.sum(packed * pick_ref[0], axis=1, keepdims=True)


def dot_turned(left, right):
    return lax.dot_general(left, right, (((1,), (1,)), ((), ())), preferred_element_type=F32)


def clear_first(*refs):
    @pl.when(pl.program_id(1) == 0)
    def _():
        for ref in refs:
            ref[...] = jnp.zeros_like(ref)


def join_weights(in_ref, join_ref):
    hidden = in_ref.shape[3]
    join_ref[:, :hidden] = in_ref[0, 0]
    join_ref[:, hidden:] = in_ref[1, 0]


def expert_forward_kernel(rows_ref, pick_ref, in_ref, out_ref, partial_ref, acc_ref):
    width = out_ref.shape[2]
    clear_first(acc_ref)
    rows = rows_ref[:, :width]
    gate_proj = jnp.dot(rows, in_ref[0, 0], preferred_element_type=F32)
    up_proj = jnp.dot(rows, in_ref[1, 0], preferred_element_type=F32)
    _, _, hidden = gated(gate_proj, up_proj)
    weighted = (hidden * own_gates(rows_ref, pick_ref, width)).astype(BF16)
    acc_ref[...] += jnp.dot(weighted, out_ref[0], preferred_element_type=F32)

    @pl.when(pl.program_id(1) == pl.num_programs(1) - 1)
    def _():
        partial_ref[...] = acc_ref[...].astype(BF16)


def expert_grads(
    gate_proj, up_proj, gates, upstream, join_ref, out_ref, acc_ref, gate_acc_ref, place
):
    sigmoid_gate, silu_gate, hidden = gated(gate_proj, up_proj)
    grad_raw = dot_turned(upstream, out_ref[0])
    gate_acc_ref[...] += jnp.sum(hidden * grad_raw, axis=1, keepdims=True) * place
    grad_hidden = grad_raw * gates
    grad_gate = (
        grad_hidden * up_proj * sigmoid_gate * (1.0 + gate_proj * (1.0 - sigmoid_gate))
    ).astype(BF16)
    grad_up = (grad_hidden * silu_gate).astype(BF16)
    acc_ref[...] += dot_turned(jnp.concatenate([grad_gate, grad_up], axis=1), join_ref[...])
    return grad_gate, grad_up, (hidden * gates).astype(BF16)


def store_last(partial_ref, acc_ref, gate_acc_ref):
    @pl.when(pl.program_id(1) == pl.num_programs(1) - 1)
    def _():
        width = acc_ref.shape[1]
        partial_ref[:, :width] = acc_ref[...].astype(BF16)
        partial_ref[:, width:] = gate_acc_ref[...].astype(BF16)


def expert_both_kernel(
    rows_ref,
    upstream_ref,
    pick_ref,
    place_ref,
    in_ref,
    out_ref,
    joined_ref,
    weighted_ref,
    partial_ref,
    acc_ref,
    gate_acc_ref,
    join_ref,
):
    width = out_ref.shape[2]
    hidden = out_ref.shape[1]
    join_weights(in_ref, join_ref)
    clear_first(acc_ref, gate_acc_ref)
    both = jnp.dot(rows_ref[:, :width], join_ref[...], preferred_element_type=F32)
    gate_proj, up_proj = both[:, :hidden], both[:, hidden:]
    joined_ref[0, 0] = gate_proj.astype(BF16)
    joined_ref[0, 1] = up_proj.astype(BF16)
    gates = own_gates(rows_ref, pick_ref, width)
    _, _, weighted_ref[0] = expert_grads(
        gate_proj,
        up_proj,
        gates,
        upstream_ref[...],
        join_ref,
        out_ref,
        acc_ref,
        gate_acc_ref,
        place_ref[0],
    )
    store_last(partial_ref, acc_ref, gate_acc_ref)


def expert_back_kernel(
    rows_ref,
    upstream_ref,
    pick_ref,
    place_ref,
    in_ref,
    out_ref,
    joined_ref,
    grads_ref,
    partial_ref,
    acc_ref,
    gate_acc_ref,
    join_ref,
):
    width = out_ref.shape[2]
    hidden = out_ref.shape[1]
    join_weights(in_ref, join_ref)
    clear_first(acc_ref, gate_acc_ref)
    gates = own_gates(rows_ref, pick_ref, width)
    grads_ref[0, 0], grads_ref[0, 1], _ = expert_grads(
        joined_ref[0, 0].astype(F32),
        joined_ref[0, 1].astype(F32),
        gates,
        upstream_ref[...],
        join_ref,
        out_ref,
        acc_ref,
        gate_acc_ref,
        place_ref[0],
    )
    store_last(partial_ref, acc_ref, gate_acc_ref)


def expert_call(kernel, name, rows, upstream, weights, extra_in=(), outs=(), grads=True):
    w_in, w_out = weights["w_in"], weights["w_out"]
    _, experts, width, hidden = w_in.shape
    token_count, total = rows.shape
    extra = total - width
    block = min(token_count, 512)

    def per_expert(*lead):
        zeros = (0,) * len(lead)
        return (
            jax.ShapeDtypeStruct((experts,) + lead + (token_count, hidden), BF16),
            pl.BlockSpec((1,) + lead + (block, hidden), lambda t, e: (e,) + zeros + (t, 0)),
        )

    def row_block(columns):
        return pl.BlockSpec((block, columns), lambda t, e: (t, 0))

    lane = pl.BlockSpec((1, 1, extra), lambda t, e: (e, 0, 0))
    out_width = total if grads else width
    outputs = [per_expert(*lead) for lead in outs] + [
        (jax.ShapeDtypeStruct((token_count, out_width), BF16), row_block(out_width))
    ]
    first = [rows] + ([upstream] if grads else [])
    marks = [weights["pick"]] + ([weights["place"]] if grads else [])
    return pl.pallas_call(
        kernel,
        out_shape=[shape for shape, _ in outputs],
        grid=(token_count // block, experts),
        in_specs=[row_block(array.shape[1]) for array in first]
        + [lane] * len(marks)
        + [
            pl.BlockSpec((2, 1, width, hidden), lambda t, e: (0, e, 0, 0)),
            pl.BlockSpec((1, hidden, width), lambda t, e: (e, 0, 0)),
        ]
        + [per_expert(2)[1] for _ in extra_in],
        out_specs=[spec for _, spec in outputs],
        scratch_shapes=[pltpu.VMEM((block, width), F32)]
        + (
            [pltpu.VMEM((block, extra), F32), pltpu.VMEM((width, 2 * hidden), BF16)]
            if grads
            else []
        ),
        compiler_params=pltpu.CompilerParams(vmem_limit_bytes=60 << 20),
        name=name,
    )(*first, *marks, w_in, w_out, *extra_in)


def body(
    x_in,
    cotangent,
    segments,
    routes,
    norm1_gain,
    norm2_gain,
    q_gain,
    k_gain,
    w_qkv,
    w_o,
    router,
    w_in,
    w_out,
):
    section_index = lax.axis_index("section")
    expert_index = lax.axis_index("expert")
    head_index = lax.axis_index("head")
    groups = lax.axis_size("expert")
    first_section = 0
    last_section = lax.axis_size("section") - 1
    on_first = section_index == first_section
    layer_start = x_in[0]
    token_count, model_width = layer_start.shape
    head_dim = q_gain.shape[1]
    expert_count = router.shape[2]
    local_experts = w_in.shape[1]
    width_part = norm1_gain.shape[1]
    head_width = w_o.shape[1]
    lane_pad = -expert_count % 64
    extra = 2 * (expert_count + lane_pad)

    shared = jnp.concatenate(
        [norm1_gain, norm2_gain, router[0].astype(F32).T], axis=0
    )
    shared = lax.all_gather(shared, "head", axis=1, tiled=True)
    router_wide = shared[2:].T
    router_full = router_wide.astype(BF16)
    weights = {
        "gain_one": shared[0],
        "gain_two": shared[1],
        "q_gain": q_gain,
        "k_gain": k_gain,
        "w_qkv": w_qkv[0],
        "w_o": w_o[0],
        "w_out": w_out[0],
    }
    tables = block_layout(segments[0, 0], head_dim)
    columns = jnp.arange(expert_count, dtype=jnp.int32)
    chosen = jnp.any(routes[0, 0][:, :, None] == columns[None, None, :], axis=1)
    lanes = jnp.arange(extra, dtype=jnp.int32)[None, None, :]
    own_experts = expert_index * local_experts + jnp.arange(local_experts, dtype=jnp.int32)
    weights["pick"] = (lanes % (extra // 2) == own_experts[:, None, None]).astype(F32)
    weights["place"] = (lanes == own_experts[:, None, None]).astype(F32)

    slab = model_width // groups

    def slabs(array):
        return [
            lax.dynamic_slice_in_dim(array, (expert_index + r) % groups * slab, slab, 1)
            for r in range(groups)
        ]

    def early_blocks(saved):
        return [jnp.concatenate([block, saved[2][3]], axis=1) for block in slabs(saved[0])]

    def layer_forward(layer_in, section, earlier, beside=None):
        partial, saved = attention_forward(layer_in, tables, weights)
        if beside is not None:
            partial, beside = lax.optimization_barrier((partial, beside))
        attention_sum = head_sum(partial, section)
        if earlier is not None:
            beside = spread_section(early_blocks(saved), first_section)
            attention_sum, beside = lax.optimization_barrier((attention_sum, beside))
            attention_sum = jnp.where(on_first, earlier[0], attention_sum)
        middle = layer_in.astype(F32) + attention_sum
        normed = rms_scale(middle, weights["gain_two"]).astype(BF16)
        probs = route_probabilities(normed, router_full)
        high, low = split_pair(jnp.where(chosen, probs, 0.0))
        pad = jnp.zeros((token_count, lane_pad), F32)
        sent = jnp.concatenate(
            [normed] + [part.astype(BF16) for part in (high, pad, low, pad)], axis=1
        )
        if earlier is None:
            sent, one = lax.optimization_barrier((sent, jnp.ones((1, 1, 1, 1), BF16)))
            weights["w_in"] = jnp.transpose(w_in[0] * one, (2, 0, 1, 3))
        rows = jnp.concatenate(group_rows(sent, section))
        if earlier is not None:
            rows = jnp.where(on_first, earlier[1], rows)
        return (attention_sum, rows), saved, (middle, normed, probs), beside

    def layer_output(middle, mixed, section):
        mixed = group_sum(jnp.split(mixed, groups), section)
        return (middle + head_sum(mixed, section)).astype(BF16)

    def own_width(array, axis):
        return lax.dynamic_slice_in_dim(array, head_index * width_part, width_part, axis)

    def layer_backward(partial, experts, grad_all, saved, kept, layer_in, section, earlier):
        normed_one, projected, rotated = saved
        middle, normed, probs = kept
        summed = group_sum(jnp.split(partial, groups), section)
        expert_sums = None
        if earlier is None:
            summed, expert_sums = lax.optimization_barrier((summed, experts))
        else:
            expert_sums = weight_grads(*experts, grad_all)
            first_blocks, later_blocks = earlier[2]
            summed, expert_sums, later_blocks = lax.optimization_barrier(
                (summed, expert_sums, later_blocks)
            )
            later_blocks = spread_section(later_blocks, last_section)
        total = head_sum(summed, section)
        if earlier is not None:
            total = jnp.where(on_first, total, earlier[0])
        upstream = grad_all[:token_count].astype(F32)
        grad_probs = jnp.where(chosen, total[:, model_width : model_width + expert_count], 0.0)
        grad_logit = probs * (grad_probs - jnp.sum(probs * grad_probs, axis=-1, keepdims=True))
        grad_norm = total[:, :model_width] + jnp.dot(
            grad_logit, router_wide.T, precision=lax.Precision.HIGHEST
        )
        _, pull_two = jax.vjp(rms_scale, middle, weights["gain_two"])
        grad_mid_norm, gain_two_grad = pull_two(grad_norm)
        grad_middle = upstream + grad_mid_norm
        grad_narrow = grad_middle.astype(BF16)
        router_part = jnp.dot(
            grad_logit.T, own_width(normed, 1).astype(F32), precision=lax.Precision.HIGHEST
        )
        router_part = jnp.concatenate([router_part, own_width(gain_two_grad, 0)[None]])
        if earlier is not None:
            grad_narrow, router_part = lax.optimization_barrier((grad_narrow, router_part))
        grad_att = lax.dot_general(
            grad_narrow, weights["w_o"], (((1,), (1,)), ((), ())), preferred_element_type=F32
        ).astype(BF16)
        grad_proj, q_grad, k_grad = attend_back(projected, tables, weights, rotated, grad_att)
        wide_proj = jnp.concatenate(list(grad_proj), axis=1)
        grad_blocks = [jnp.concatenate([block, wide_proj], axis=1) for block in slabs(grad_narrow)]
        if earlier is not None:
            grad_blocks = spread_section(grad_blocks, section)
        partial_one = jnp.einsum(
            "ise,ide->sd", grad_proj, weights["w_qkv"], preferred_element_type=F32
        )
        wide_in = layer_in.astype(F32)
        own_norm = wide_in * lax.rsqrt(
            jnp.mean(wide_in * wide_in, axis=-1, keepdims=True) + NORM_EPSILON
        )
        gain_one_part = jnp.sum(partial_one * own_norm, axis=0, keepdims=True)
        gain_pair = jnp.concatenate([q_grad, k_grad], axis=1)
        gain_pair = jnp.pad(gain_pair, ((0, 0), (0, model_width - 2 * head_dim)))
        tail_rows = split_pair(gain_one_part) + split_pair(gain_pair)
        tail_rows = jnp.pad(jnp.concatenate(tail_rows), ((0, 16 - len(tail_rows)), (0, 0)))
        total_one = head_sum(jnp.concatenate([partial_one, tail_rows]), section)
        if earlier is not None:
            total_one = jnp.where(on_first, total_one, earlier[1])
            grad_blocks = [
                jnp.where(on_first, jnp.concatenate([a, b], axis=1), c)
                for a, b, c in zip(grad_blocks, first_blocks, later_blocks)
            ]
        _, pull_one = jax.vjp(rms_scale, wide_in, weights["gain_one"])
        grad_x_norm, _ = pull_one(total_one[:token_count])
        result = (grad_middle + grad_x_norm).astype(BF16)
        return (total, total_one, grad_blocks), result, router_part, expert_sums

    cotangent_all = jnp.concatenate(group_rows(cotangent[0], last_section))
    exchanged, _, kept, cotangent_all = layer_forward(
        layer_start, first_section, None, cotangent_all
    )
    (mixed,) = expert_call(
        expert_forward_kernel, "experts", exchanged[1], None, weights, grads=False
    )
    first_result = layer_output(kept[0], mixed, first_section)
    arrived = move(first_result, first_section, last_section)
    layer_in = jnp.where(on_first, layer_start, arrived)
    exchanged, saved, kept, first_blocks = layer_forward(layer_in, last_section, exchanged)
    rows = exchanged[1]
    joined, weighted, partial = expert_call(
        expert_both_kernel,
        "experts_both",
        rows,
        cotangent_all,
        weights,
        outs=((2,), ()),
    )
    mixed = jnp.einsum(
        "etf,efd->td", weighted, weights["w_out"], preferred_element_type=F32
    ).astype(BF16)
    exchanged, grad_result, _, (rows_turned, mixed) = layer_backward(
        partial, (rows[:, :model_width].T, mixed), cotangent_all, saved, kept, layer_in, last_section, None
    )
    later = [
        jnp.concatenate([a, b], axis=1) for a, b in zip(exchanged[2], early_blocks(saved))
    ]
    exchanged = exchanged[:2] + ((first_blocks, later),)
    arrived_all = jnp.concatenate(
        [move(grad_result, last_section, first_section, expert_shift=r) for r in range(groups)]
    )
    mixed, arrived_all = lax.optimization_barrier((mixed, arrived_all))
    last_mixed = group_sum(jnp.split(mixed, groups), last_section)
    grad_all = jnp.where(on_first, arrived_all, cotangent_all)
    grad_joined, partial = expert_call(
        expert_back_kernel,
        "experts_back",
        rows,
        grad_all,
        weights,
        extra_in=(joined,),
        outs=((2,),),
    )
    partial, last_mixed = lax.optimization_barrier((partial, last_mixed))
    exchanged, grad_result, router_part, (grad_w_in, grad_w_out) = layer_backward(
        partial,
        (rows_turned, grad_joined, weighted),
        grad_all,
        saved,
        kept,
        layer_in,
        first_section,
        exchanged,
    )

    last_mixed, _ = lax.optimization_barrier((last_mixed, exchanged[0]))
    last_result = (kept[0] + head_sum(last_mixed, last_section)).astype(BF16)
    layer_result = jnp.where(on_first, first_result, last_result)
    tail_rows = exchanged[1][token_count:]
    gains_own = jnp.concatenate(
        [
            own_width(tail_rows[0] + tail_rows[1], 0),
            (tail_rows[2] + tail_rows[3])[: 2 * head_dim],
            router_part.reshape(-1),
        ]
    ).reshape(-1, 128)
    grad_blocks, _ = lax.optimization_barrier((exchanged[2], gains_own))
    gains_parts = jnp.stack(spread([gains_own] * groups))
    gains_order = (expert_index - jnp.arange(groups, dtype=jnp.int32)) % groups
    gains_sum = jnp.sum(gains_parts[gains_order], axis=0).reshape(-1)
    router_sum = gains_sum[width_part + 2 * head_dim :].reshape(expert_count + 1, width_part)
    grad_rows = jnp.concatenate(grad_blocks)
    proj_end = slab + 3 * head_width
    slab_rows = grad_rows[:, proj_end : proj_end + slab]
    attended_rows = grad_rows[:, proj_end + slab :]
    grad_w_o = jnp.einsum(
        "te,td->ed", attended_rows, grad_rows[:, :slab], preferred_element_type=F32
    )
    grad_w_qkv = jnp.stack(
        [
            jnp.einsum("td,te->de", slab_rows, part, preferred_element_type=F32)
            for part in jnp.split(grad_rows[:, slab:proj_end], 3, axis=1)
        ]
    )
    return (
        layer_result[None, None],
        grad_result[None, None],
        gains_sum[None, :width_part],
        router_sum[expert_count:],
        gains_sum[None, width_part : width_part + head_dim],
        gains_sum[None, width_part + head_dim : width_part + 2 * head_dim],
        grad_w_qkv[None],
        grad_w_o[None],
        router_sum[:expert_count].T[None],
        grad_w_in[None],
        grad_w_out[None],
    )


def solution(mesh):
    placed = (
        P(None, "expert", None),
        P(None, "expert", None),
        P(None, "expert", None),
        P("section", None, "expert", None),
        P("section", "head"),
        P("section", "head"),
        P("section", None),
        P("section", None),
        P("section", None, None, "head"),
        P("section", "head", None),
        P("section", "head", None),
        P("section", "expert", None, None, "head"),
        P("section", "expert", "head", None),
    )
    return jax.shard_map(
        body,
        mesh=mesh,
        in_specs=placed,
        out_specs=(
            P("section", None, "expert", None),
            P("section", None, "expert", None),
            P("section", "head"),
            P("section", "head"),
            P("section", None),
            P("section", None),
            P("section", None, "expert", "head"),
            P("section", "head", "expert"),
            P("section", "head", None),
            P("section", "expert", None, None, "head"),
            P("section", "expert", "head", None),
        ),
        check_vma=False,
    )
```
